1024 devices in a mesh: dp: 64 (over y_hi, z), fsdp: 16 (over y_lo, x, core).
Axes of the slice: x: 4, y: 8 (y_hi: 4, y_lo: 2; y = y_hi * 2 + y_lo), z: 16, core: 2. Of those that a mesh axis runs over, the one named last changes fastest.
Arguments:
- features: bfloat16 [401408, 512], P(('dp', 'fsdp')), may hold values from -6 to 6
- shortcut: bfloat16 [401408, 2048], P(('dp', 'fsdp')), may hold values from -6 to 6
- conv_weight: bfloat16 [2048, 512], P('fsdp'), may hold values from -0.25 to 0.25
- proj_weight: bfloat16 [2048, 256], P('fsdp'), may hold values from -0.125 to 0.125
- partner: int32 [8192], P(('dp', 'fsdp')), may hold values from 0 to 511, as said below
Outputs:
- grad_conv: float32 [2048, 512], P('fsdp')
- grad_proj: float32 [2048, 256], P('fsdp')
- group_loss: float32 [16], P('fsdp')
The draws below stay inside these ranges and needn't reach their ends.
Inputs may be any that keep to these rules, and one draw needn't show every extreme that they name: Each image's partner is another image of its group, given as its member index, and the pairing is mutual: the partner of the partner is the image itself.
All inputs are finite; a program needn't handle non-finite values.
Results may differ from the reference program's by a relative error of at most 0.035.
Values may be sent and summed in bfloat16 or wider, within the bound.
A program may use at most 32 MiB of HBM per device.

```python
import jax
import jax.numpy as jnp
from jax import lax

C_IN = 512
C_OUT = 2048
EMB = 256
POS = 49
IMG_DEV = 8
ROWS = 392
GROUP = 512
IMAGES = 8192
N_DP = 64
N_FSDP = 16


def draw_partner(key, part):
    key_list = jax.random.split(key, N_FSDP)

    def one_group(group_key):
        shuffled = jax.random.permutation(group_key, GROUP)
        couples = shuffled.reshape(GROUP // 2, 2).astype(jnp.int32)
        partner_of = jnp.zeros((GROUP,), jnp.int32)
        partner_of = partner_of.at[couples[:, 0]].set(couples[:, 1])
        partner_of = partner_of.at[couples[:, 1]].set(couples[:, 0])
        return partner_of
    grouped = jax.vmap(one_group)(key_list)
    return grouped.reshape(N_FSDP, N_DP, IMG_DEV).transpose(1, 0, 2).reshape(N_DP * N_FSDP * IMG_DEV)


def level_of(stream_key, dims, cuts, low, high):
    level, own = 1.0, jax.random.fold_in(stream_key, 6)
    for position, parts in cuts:
        steps = jnp.exp(jax.random.uniform(jax.random.fold_in(own, position), (parts,), jnp.float32, low / len(cuts), high / len(cuts)))
        level = level * jnp.repeat(steps, dims[position] // parts).reshape([-1 if axis == position else 1 for axis in range(len(dims))])
    return level


def normal_values(key, shape, scale, bound, shards=(), kind=jnp.bfloat16):
    array = scale * jax.random.normal(key, shape, jnp.float32)
    if shards:
        array = array * level_of(key, shape, shards, -0.22, 0.18)
    return jnp.clip(array, -bound, bound).astype(kind)


def setup_inputs(seed: int = 0) -> dict:
    keys = jax.random.split(jax.random.key(seed), 6)
    features = normal_values(keys[0], (IMAGES * POS, C_IN), 1.0, 6.0, ((0, 1024),))
    shortcut = normal_values(keys[1], (IMAGES * POS, C_OUT), 1.0, 6.0, ((0, 1024),))
    conv_weight = normal_values(keys[2], (C_OUT, C_IN), C_IN ** -0.5, 0.25, ((0, 16),))
    proj_weight = normal_values(keys[3], (C_OUT, EMB), C_OUT ** -0.5, 0.125, ((0, 16),))
    partner = draw_partner(jax.random.fold_in(keys[5], 71), 0)
    return {"features": features, "shortcut": shortcut, "conv_weight": conv_weight, "proj_weight": proj_weight, "partner": partner}


gamma_weight = 3.0
epsilon = 1e-06

def conv_preact(feat_block, short_block, conv_weight):
    return lax.dot_general(feat_block, conv_weight, (((1,), (1,)), ((), ())), preferred_element_type=jnp.float32) + short_block.astype(jnp.float32)

def pool_rows(hidden):
    return lax.optimization_barrier(jnp.mean(hidden.reshape(IMG_DEV, POS, hidden.shape[-1]), axis=1))

def group_terms(embed_group, partner_group):
    count = embed_group.shape[0]
    center = lax.optimization_barrier(jnp.mean(embed_group, axis=0))
    spread = 2.0 * jnp.mean(lax.optimization_barrier(jnp.sum((embed_group - center) ** 2, axis=1)))
    squares = lax.optimization_barrier(jnp.sum(embed_group * embed_group, axis=1))
    inner = jnp.dot(embed_group, embed_group.T, precision=lax.Precision.HIGHEST)
    kernel = jnp.exp(-(squares[:, None] + squares[None, :] - 2.0 * inner) / (2.0 * spread))
    row_mean = lax.optimization_barrier(jnp.mean(kernel, axis=1))
    total_mean = jnp.mean(row_mean)
    centered = kernel - row_mean[:, None] - row_mean[None, :] + total_mean
    scale_sq = float(count - 1) ** 2
    root = jnp.sqrt(jnp.sum(centered * centered) / scale_sq + epsilon)
    onehot = (partner_group[:, None] == jnp.arange(count, dtype=jnp.int32)[None, :]).astype(jnp.float32)
    positive = jnp.sum(kernel * onehot) / count
    loss_value = -(positive - total_mean) + gamma_weight * root
    coeff = (-onehot / count + 1.0 / (count * count) + gamma_weight * centered / (scale_sq * root)) / N_FSDP
    weighted = coeff * kernel
    grad_embed = -(2.0 / spread) * (lax.optimization_barrier(jnp.sum(weighted, axis=1))[:, None] * embed_group - jnp.dot(weighted, embed_group, precision=lax.Precision.HIGHEST))
    return (loss_value, grad_embed)

def reference(features, shortcut, conv_weight, proj_weight, partner):
    blocks = N_DP * N_FSDP
    feat_blocks = features.reshape(blocks, ROWS, C_IN)
    short_blocks = shortcut.reshape(blocks, ROWS, C_OUT)

    def forward_block(operands):
        feat_block, short_block = operands
        hidden = jnp.maximum(conv_preact(feat_block, short_block, conv_weight), 0.0)
        return pool_rows(hidden).astype(jnp.bfloat16)
    pooled = lax.map(forward_block, (feat_blocks, short_blocks))
    embed = jnp.dot(pooled.reshape(IMAGES, C_OUT), proj_weight, preferred_element_type=jnp.float32)
    embed_groups = embed.reshape(N_DP, N_FSDP, IMG_DEV, EMB).transpose(1, 0, 2, 3).reshape(N_FSDP, GROUP, EMB)
    partner_groups = partner.reshape(N_DP, N_FSDP, IMG_DEV).transpose(1, 0, 2).reshape(N_FSDP, GROUP)
    losses, grad_groups = lax.map(lambda operands: group_terms(operands[0], operands[1]), (embed_groups, partner_groups))
    grad_embed = grad_groups.reshape(N_FSDP, N_DP, IMG_DEV, EMB).transpose(1, 0, 2, 3).astype(jnp.bfloat16)
    feat_grid = features.reshape(N_DP, N_FSDP, ROWS, C_IN)
    short_grid = shortcut.reshape(N_DP, N_FSDP, ROWS, C_OUT)
    pooled_grid = pooled.reshape(N_DP, N_FSDP, IMG_DEV, C_OUT)

    def device_term(operands):
        feat_block, short_block, pooled_block, grad_block = operands
        preact = conv_preact(feat_block, short_block, conv_weight)
        grad_pool = jnp.dot(grad_block, proj_weight.T, preferred_element_type=jnp.float32) / POS
        spread_rows = jnp.repeat(grad_pool, POS, axis=0)
        grad_hidden = jnp.where(preact > 0, spread_rows, 0.0).astype(jnp.bfloat16)
        conv_part = lax.dot_general(grad_hidden, feat_block, (((0,), (0,)), ((), ())), preferred_element_type=jnp.float32)
        proj_part = lax.dot_general(pooled_block, grad_block, (((0,), (0,)), ((), ())), preferred_element_type=jnp.float32)
        return jnp.concatenate([conv_part, proj_part], axis=1).astype(jnp.bfloat16)

    def add_slab(running, slab):
        terms = lax.map(device_term, slab)
        return (running + lax.optimization_barrier(jnp.sum(terms.astype(jnp.float32), axis=0)), None)
    start_total = jnp.zeros((C_OUT, C_IN + EMB), jnp.float32)
    total, _ = lax.scan(add_slab, start_total, (feat_grid, short_grid, pooled_grid, grad_embed))
    return (total[:, :C_IN], total[:, C_IN:], losses.astype(jnp.float32))
```

```python
import jax
import jax.numpy as jnp
from jax import lax
from jax.experimental import pallas as pl
from jax.experimental.pallas import tpu as pltpu
from jax.sharding import PartitionSpec as P

MESH = pl.DeviceIdType.MESH
HIGH = lax.Precision.HIGHEST
BF16 = jnp.bfloat16
F32 = jnp.float32

POS = 49
GAMMA = 3.0
EPSILON = 1e-06

YH, ZH, ZL = 4, 4, 4
YL, X = 2, 4


def dot(a, b, dims=((1,), (0,)), precision=None):
    return lax.dot_general(
        a, b, (dims, ((), ())), precision=precision, preferred_element_type=F32
    )


def kernel(
    feat_h, short_h, conv_h, proj_h, partner_s,
    oconv, oproj, oloss,
    feat, short, featT, W, PW, hid, pooled, part, emb, zbuf, kmat, rcol,
    term, core_in, pair_sum, group_in,
    red0, red0_in, red1, red1_in, red2, fin,
    lsem, ssem, rsem,
):
    chips = YL * X
    dp = YH * ZH * ZL
    images = 8
    width = feat.shape[1]
    emb_w = emb.shape[2]
    group = dp * images

    d = lax.axis_index("dp")
    f = lax.axis_index("fsdp")
    yh = lax.div(d, ZH * ZL)
    zh = lax.rem(lax.div(d, ZL), ZH)
    zl = lax.rem(d, ZL)
    chip = lax.div(f, 2)
    yl = lax.div(chip, X)
    x = lax.rem(chip, X)
    c = lax.rem(f, 2)

    def dev_chip(ch, core):
        return (d, ch * 2 + core)

    def dev_dp(a, b, e):
        return ((a * ZH + b) * ZL + e, f)

    used = [0]
    pending = []

    def send(src, dst, dev):
        i = used[0]
        used[0] += 1
        copy = pltpu.make_async_remote_copy(
            src_ref=src, dst_ref=dst, send_sem=ssem.at[i], recv_sem=rsem.at[i],
            device_id=dev, device_id_type=MESH,
        )
        copy.start()
        pending.append(copy)
        return copy

    offsets = [(dy, dx) for dy in range(YL) for dx in range(X)]
    offsets.sort(key=lambda o: (o[0] + min(o[1], X - o[1]), o[0]))

    def to_chip(o):
        return lax.rem(yl + o[0], YL) * X + lax.rem(x + o[1], X)

    def from_chip(o):
        return lax.rem(yl + YL - o[0], YL) * X + lax.rem(x + X - o[1], X)

    mine = pl.ds(pl.multiple_of(c * 128, 128), 128)
    local = [
        pltpu.make_async_copy(conv_h, W.at[chip, mine], lsem.at[0]),
        pltpu.make_async_copy(feat_h, feat, lsem.at[1]),
        pltpu.make_async_copy(short_h, short, lsem.at[2]),
        pltpu.make_async_copy(proj_h, PW.at[chip, mine], lsem.at[3]),
    ]
    for copy in local:
        copy.start()

    peers = [dev_chip(chip, 1 - c)]
    peers += [dev_chip(to_chip(o), c) for o in offsets[1:]]
    peers += [dev_dp(lax.rem(yh + j, YH), zh, zl) for j in range(1, YH)]
    peers += [dev_dp(yh, lax.rem(zh + j, ZH), zl) for j in range(1, ZH)]
    peers += [dev_dp(yh, zh, lax.rem(zl + j, ZL)) for j in range(1, ZL)]
    barrier = pltpu.get_barrier_semaphore()
    for peer in peers:
        pl.semaphore_signal(barrier, inc=1, device_id=peer, device_id_type=MESH)

    slot = (zl * YH + yh) * ZH + zh
    row8 = lax.broadcasted_iota(jnp.int32, (images, 128), 0)
    column = jnp.zeros((images, 128), jnp.int32)
    for i in range(images):
        column = jnp.where(row8 == i, partner_s[i], column)
    part[pl.ds(slot, 1)] = column.astype(F32)[None]

    pl.semaphore_wait(barrier, len(peers))

    other = dev_chip(chip, 1 - c)
    conv_direct = {}
    for o in offsets[1:]:
        conv_direct[o] = send(conv_h, W.at[chip, mine], dev_chip(to_chip(o), c))
    conv_pair = {offsets[0]: send(conv_h, W.at[chip, mine], other)}

    def dp_stage(buf, stage):
        if stage == 0:
            base, size, n = slot, 1, ZH
            dev = lambda j: dev_dp(yh, lax.rem(zh + j, ZH), zl)
        elif stage == 1:
            base, size, n = (zl * YH + yh) * ZH, ZH, YH
            dev = lambda j: dev_dp(lax.rem(yh + j, YH), zh, zl)
        else:
            base, size, n = zl * YH * ZH, YH * ZH, ZL
            dev = lambda j: dev_dp(yh, zh, lax.rem(zl + j, ZL))
        view = buf.at[pl.ds(base, size)]
        return [send(view, view, dev(j)) for j in range(1, n)]

    def arrive(copies):
        for copy in copies:
            copy.wait_recv()

    part_copies = dp_stage(part, 0)
    proj_direct = {}
    for o in offsets[1:]:
        proj_direct[o] = send(proj_h, PW.at[chip, mine], dev_chip(to_chip(o), c))
    proj_pair = {offsets[0]: send(proj_h, PW.at[chip, mine], other)}

    ri = lax.broadcasted_iota(jnp.int32, (images, images * POS), 1)
    ii = lax.broadcasted_iota(jnp.int32, (images, images * POS), 0)
    pool_mat = jnp.where((ri >= ii * POS) & (ri < ii * POS + POS), 1.0, 0.0).astype(BF16)
    ri = lax.broadcasted_iota(jnp.int32, (images * POS, images), 0)
    ii = lax.broadcasted_iota(jnp.int32, (images * POS, images), 1)
    spread_mat = jnp.where((ri >= ii * POS) & (ri < ii * POS + POS), 1.0, 0.0).astype(BF16)

    def lanes(kk):
        return pl.ds(pl.multiple_of(kk * 256, 256), 256)

    def forward(kk):
        pre = dot(feat[...], W[kk], ((1,), (1,))) + short[:, lanes(kk)].astype(F32)
        h = jnp.maximum(pre, 0.0)
        hi = h.astype(BF16)
        low = (h - hi.astype(F32)).astype(BF16)
        hid[kk] = hi
        total = dot(pool_mat, hi) + dot(pool_mat, low)
        pooled[kk] = (total / POS).astype(BF16)

    for copy in local[:3]:
        copy.wait()
    for n, o in enumerate(offsets):
        if n:
            src = from_chip(o)
            conv_direct[o].wait_recv()
            view = W.at[src, mine]
            conv_pair[o] = send(view, view, other)
            last = offsets[n - 1]
            conv_pair[last].wait_recv()
            forward(from_chip(last))
        if n == min(1, chips - 1):
            featT[...] = jnp.transpose(feat[...].astype(F32)).astype(BF16)
    arrive(part_copies)
    part_copies = dp_stage(part, 1)
    for n, o in enumerate(offsets[1:]):
        src = from_chip(o)
        proj_direct[o].wait_recv()
        view = PW.at[src, mine]
        proj_pair[o] = send(view, view, other)
    conv_pair[offsets[-1]].wait_recv()
    forward(from_chip(offsets[-1]))
    local[3].wait()
    arrive(part_copies)
    part_copies = dp_stage(part, 2)

    own = jnp.zeros((images, emb_w), F32)
    for o in offsets:
        proj_pair[o].wait_recv()
        kk = from_chip(o)
        own = own + dot(pooled[kk], PW[kk])

    emb[pl.ds(slot, 1)] = own[None]
    for stage in range(3):
        arrive(dp_stage(emb, stage))
    arrive(part_copies)

    zall = emb[...].reshape(group, emb_w)
    center = jnp.mean(zall, axis=0, keepdims=True)
    zc = zall - center
    zbuf[...] = zc
    square = zc * zc
    spread = 2.0 * jnp.sum(square) / group
    sq_row = dot(jnp.ones((8, emb_w), F32), square, ((1,), (1,)), HIGH)[0:1]
    lane = lax.broadcasted_iota(jnp.int32, (1, group), 1)
    ls = lane // images
    lzl = ls // (YH * ZH)
    lyh = (ls // ZH) % YH
    lzh = ls % ZH
    member = (((lyh * ZH + lzh) * ZL + lzl) * images + lane % images).astype(F32)

    step = 64 if group % 64 == 0 else group
    scale = 1.0 / (2.0 * spread)

    def kernel_rows(i, carry):
        col_sum, positive = carry
        rows = pl.ds(pl.multiple_of(i * (step // images), step // images), step // images)
        at = pl.ds(pl.multiple_of(i * step, step), step)
        z = zbuf[at, :]
        inner = dot(z, zbuf[...], ((1,), (1,)), HIGH)
        sq = jnp.sum(z * z, axis=1, keepdims=True)
        kk = jnp.exp(-(sq + sq_row - 2.0 * inner) * scale)
        kmat[at, :] = kk
        rcol[at, :] = jnp.broadcast_to(jnp.mean(kk, axis=1, keepdims=True), (step, 128))
        who = part[rows].reshape(step, 128)[:, 0:1]
        positive = positive + jnp.sum(jnp.where(who == member, kk, 0.0), axis=0, keepdims=True)
        return col_sum + jnp.sum(kk, axis=0, keepdims=True), positive

    zero = jnp.zeros((1, group), F32)
    col_sum, positive = lax.fori_loop(0, group // step, kernel_rows, (zero, zero))
    row_mean = col_sum / group
    t = jnp.sum(row_mean) / group

    def square_rows(i, carry):
        at = pl.ds(pl.multiple_of(i * step, step), step)
        cen = kmat[at, :] - rcol[at, 0:1] - row_mean + t
        return carry + jnp.sum(cen * cen, axis=0, keepdims=True)

    sums = lax.fori_loop(0, group // step, square_rows, zero)
    scale_sq = float(group - 1) ** 2
    root_v = jnp.sqrt(jnp.broadcast_to(jnp.sum(sums) / scale_sq + EPSILON, (1, 128)))
    loss = -(jnp.sum(positive) / group - t) + GAMMA * root_v
    oloss[...] = loss
    root = root_v[0:1, 0:1]

    at = pl.ds(pl.multiple_of(slot * images, images), images)
    k_own = kmat[at, :]
    cen = k_own - rcol[at, 0:1] - row_mean + t
    who = part[pl.ds(slot, 1)].reshape(images, 128)[:, 0:1]
    hot = jnp.where(who == member, 1.0, 0.0)
    coeff = (-hot / group + 1.0 / (group * group) + GAMMA * cen / (scale_sq * root)) / (chips * 2)
    weighted = coeff * k_own
    z_own = zbuf[at, :]
    grad = -(2.0 / spread) * (
        jnp.sum(weighted, axis=1, keepdims=True) * z_own
        - dot(weighted, zbuf[...], precision=HIGH)
    )
    ge = grad.astype(BF16)
    geT = jnp.transpose(ge.astype(F32)).astype(BF16)

    def backward(n, kk):
        gp = (dot(ge, PW[kk], ((1,), (1,))) / POS).astype(BF16)
        rows = dot(spread_mat, gp)
        gh = jnp.where(hid[kk].astype(F32) > 0.0, rows, 0.0).astype(BF16)
        conv_t = dot(featT[...], gh).astype(BF16)
        proj_t = dot(geT, pooled[kk]).astype(BF16)
        for half in range(2):
            cols = slice(half * 128, half * 128 + 128)
            term[n, half, 0:width] = conv_t[:, cols]
            term[n, half, width:] = proj_t[:, cols]

    order = list(reversed(offsets))
    core_copies = {}
    group_copies = []

    def pair(n):
        core_copies[n].wait_recv()
        total = term[n, pl.ds(c, 1)][0].astype(F32) + core_in[n].astype(F32)
        pair_sum[n] = total.astype(BF16)
        if n < len(order) - 1:
            group_copies.append(
                send(pair_sum.at[n], group_in.at[n], dev_chip(to_chip(order[n]), c))
            )

    for n, o in enumerate(order):
        backward(n, to_chip(o))
        core_copies[n] = send(term.at[n, 1 - c], core_in.at[n], other)
        if n:
            pair(n - 1)
    last = len(order) - 1
    pair(last)
    arrive(group_copies)
    total = pair_sum[last].astype(F32)
    for n in range(last):
        total = total + group_in[n].astype(F32)
    red0[...] = total.astype(BF16).reshape(red0.shape)

    copies = []
    for j in range(1, ZL):
        q = lax.rem(zl + j, ZL)
        copies.append(send(red0.at[q], red0_in.at[j], dev_dp(yh, zh, q)))
    arrive(copies)
    total = red0[zl].astype(F32)
    for j in range(1, ZL):
        total = total + red0_in[j].astype(F32)
    red1[...] = total.astype(BF16)
    copies = []
    for j in range(1, ZH):
        q = lax.rem(zh + j, ZH)
        copies.append(send(red1.at[q], red1_in.at[j], dev_dp(yh, q, zl)))
    arrive(copies)
    total = red1[zh].astype(F32)
    for j in range(1, ZH):
        total = total + red1_in[j].astype(F32)
    red2[yh] = total.astype(BF16)
    copies = []
    for j in range(1, YH):
        q = lax.rem(yh + j, YH)
        copies.append(send(red2.at[yh], red2.at[yh], dev_dp(q, zh, zl)))
    arrive(copies)
    total = red2[0].astype(F32)
    for j in range(1, YH):
        total = total + red2[j].astype(F32)
    fin[zl, zh] = total.astype(BF16)
    copies = []
    for j in range(1, ZH):
        q = lax.rem(zh + j, ZH)
        copies.append(send(fin.at[zl, zh], fin.at[zl, zh], dev_dp(yh, q, zl)))
    arrive(copies)
    copies = []
    for j in range(1, ZL):
        q = lax.rem(zl + j, ZL)
        copies.append(send(fin.at[zl], fin.at[zl], dev_dp(yh, zh, q)))
    arrive(copies)

    result = fin[...].astype(F32).reshape(width + emb_w, 128)
    oconv[...] = jnp.transpose(result[0:width])
    oproj[...] = jnp.transpose(result[width:])

    for copy in pending:
        copy.wait_send()


def local(features, shortcut, conv_weight, proj_weight, partner):
    rows, width = features.shape
    emb_w = proj_weight.shape[1]
    chips = YL * X
    dp = YH * ZH * ZL
    group = dp * 8
    both = width + emb_w
    piece = both // (ZL * ZH)
    sends = 2 * (chips - 1 + chips) + 2 * (YH + ZH + ZL - 3) + 2 * chips - 1
    sends += 2 * (ZL - 1 + ZH - 1) + YH - 1
    hbm = pl.BlockSpec(memory_space=pl.ANY)
    vmem = pl.BlockSpec(memory_space=pltpu.VMEM)
    grad_conv, grad_proj, loss = pl.pallas_call(
        kernel,
        out_shape=(
            jax.ShapeDtypeStruct((128, width), F32),
            jax.ShapeDtypeStruct((128, emb_w), F32),
            jax.ShapeDtypeStruct((1, 128), F32),
        ),
        in_specs=[hbm, hbm, hbm, hbm, pl.BlockSpec(memory_space=pltpu.SMEM)],
        out_specs=(vmem, vmem, vmem),
        scratch_shapes=[
            pltpu.VMEM((rows, width), BF16),
            pltpu.VMEM((rows, chips * 256), BF16),
            pltpu.VMEM((width, rows), BF16),
            pltpu.VMEM((chips, 256, width), BF16),
            pltpu.VMEM((chips, 256, emb_w), BF16),
            pltpu.VMEM((chips, rows, 256), BF16),
            pltpu.VMEM((chips, 8, 256), BF16),
            pltpu.VMEM((dp, 8, 128), F32),
            pltpu.VMEM((dp, 8, emb_w), F32),
            pltpu.VMEM((group, emb_w), F32),
            pltpu.VMEM((group, group), F32),
            pltpu.VMEM((group, 128), F32),
            pltpu.VMEM((chips, 2, both, 128), BF16),
            pltpu.VMEM((chips, both, 128), BF16),
            pltpu.VMEM((chips, both, 128), BF16),
            pltpu.VMEM((chips, both, 128), BF16),
            pltpu.VMEM((ZL, ZH, piece, 128), BF16),
            pltpu.VMEM((ZL, ZH, piece, 128), BF16),
            pltpu.VMEM((ZH, piece, 128), BF16),
            pltpu.VMEM((ZH, piece, 128), BF16),
            pltpu.VMEM((YH, piece, 128), BF16),
            pltpu.VMEM((ZL, ZH, piece, 128), BF16),
            pltpu.SemaphoreType.DMA((4,)),
            pltpu.SemaphoreType.DMA((sends,)),
            pltpu.SemaphoreType.DMA((sends,)),
        ],
        compiler_params=pltpu.CompilerParams(
            collective_id=0, has_side_effects=True, vmem_limit_bytes=48 << 20
        ),
    )(features, shortcut, conv_weight, proj_weight, partner)
    return grad_conv, grad_proj, loss[0, 0:1]


def solution(mesh):
    return jax.shard_map(
        local,
        mesh=mesh,
        in_specs=(
            P(("dp", "fsdp"), None),
            P(("dp", "fsdp"), None),
            P("fsdp", None),
            P("fsdp", None),
            P(("dp", "fsdp")),
        ),
        out_specs=(P("fsdp", None), P("fsdp", None), P("fsdp")),
        check_vma=False,
    )
```

```python
import jax
import jax.numpy as jnp
from jax import lax
from jax.experimental import pallas as pl
from jax.experimental.pallas import tpu as pltpu
from jax.sharding import PartitionSpec as P

MESH = pl.DeviceIdType.MESH
BF16 = jnp.bfloat16
F32 = jnp.float32

POS = 49
GAMMA = 3.0
EPSILON = 1e-06

YH, ZH, ZL = 4, 4, 4
YL, X = 2, 4


def far(o):
    return o[0] > 0 and o[1] > 0


def first_hop(o):
    return (o[0], 0) if o[1] in (1, X - 1) else (0, o[1])


def second_hop(o):
    return (0, o[1]) if o[1] in (1, X - 1) else (o[0], 0)


def near(n):
    return [j if j <= n // 2 else j - n for j in sorted(range(1, n), key=lambda j: min(j, n - j))]


def dot(a, b, dims=((1,), (0,)), precision=None):
    return lax.dot_general(
        a, b, (dims, ((), ())), precision=precision, preferred_element_type=F32
    )


def kernel(
    feat_h, short_h, conv_h, proj_h, partner_s,
    oconv, oproj, oloss,
    feat, short, featT, W, PW, hid, pooled, part, emb, zbuf, parts, sqs, kmat, rcol,
    term, core_in, pair_sum, group_in,
    red0, red0_in, red1, red1_in, red2, fin,
    lsem, ssem, rsem,
):
    chips = YL * X
    dp = YH * ZH * ZL
    images = 8
    width = feat.shape[1]
    emb_w = emb.shape[2]
    group = dp * images

    d = lax.axis_index("dp")
    f = lax.axis_index("fsdp")
    yh = lax.div(d, ZH * ZL)
    zh = lax.rem(lax.div(d, ZL), ZH)
    zl = lax.rem(d, ZL)
    chip = lax.div(f, 2)
    yl = lax.div(chip, X)
    x = lax.rem(chip, X)
    c = lax.rem(f, 2)

    def dev_chip(ch, core):
        return (d, ch * 2 + core)

    def dev_dp(a, b, e):
        return ((a * ZH + b) * ZL + e, f)

    used = [0]
    pending = []

    def send(src, dst, dev):
        i = used[0]
        used[0] += 1
        copy = pltpu.make_async_remote_copy(
            src_ref=src, dst_ref=dst, send_sem=ssem.at[i], recv_sem=rsem.at[i],
            device_id=dev, device_id_type=MESH,
        )
        copy.start()
        pending.append(copy)
        return copy

    offsets = [(dy, dx) for dy in range(YL) for dx in range(X)]
    offsets.sort(key=lambda o: (far(o), o[0] + min(o[1], X - o[1]), -o[0]))

    def to_chip(o):
        return lax.rem(yl + o[0], YL) * X + lax.rem(x + o[1], X)

    def from_chip(o):
        return lax.rem(yl + YL - o[0], YL) * X + lax.rem(x + X - o[1], X)

    mine = pl.ds(pl.multiple_of(c * 128, 128), 128)
    local = [
        pltpu.make_async_copy(conv_h, W.at[chip, mine], lsem.at[0]),
        pltpu.make_async_copy(feat_h, feat, lsem.at[1]),
        pltpu.make_async_copy(short_h, short, lsem.at[2]),
        pltpu.make_async_copy(proj_h, PW.at[chip, mine], lsem.at[3]),
    ]
    for copy in local:
        copy.start()

    peers = [dev_chip(chip, 1 - c)]
    peers += [dev_chip(to_chip(o), c) for o in offsets[1:] if not far(o)]
    peers += [dev_dp(lax.rem(yh + j, YH), zh, zl) for j in range(1, YH)]
    peers += [dev_dp(yh, lax.rem(zh + j, ZH), zl) for j in range(1, ZH)]
    z = zh * ZL + zl

    def dev_z(j):
        q = lax.rem(z + j + ZH * ZL, ZH * ZL)
        return (yh * ZH * ZL + q, f)

    near_z = near(ZL)
    for j in near_z:
        peers.append(dev_z(j))
    barrier = pltpu.get_barrier_semaphore()
    for peer in peers:
        pl.semaphore_signal(barrier, inc=1, device_id=peer, device_id_type=MESH)

    slot = (zl * YH + yh) * ZH + zh
    row8 = lax.broadcasted_iota(jnp.int32, (images, 128), 0)
    column = jnp.zeros((images, 128), jnp.int32)
    for i in range(images):
        column = jnp.where(row8 == i, partner_s[i], column)
    part[pl.ds(slot, 1)] = column.astype(F32)[None]

    pl.semaphore_wait(barrier, len(peers))

    other = dev_chip(chip, 1 - c)

    def block(ref, ch):
        return ref.at[ch, mine]

    def start_gather(source, ref):
        direct = {}
        for o in offsets[1:]:
            if not far(o):
                direct[o] = send(source, block(ref, chip), dev_chip(to_chip(o), c))
        return direct, {offsets[0]: send(source, block(ref, chip), other)}

    def landed(ref, o, direct, paired):
        direct[o].wait_recv()
        view = block(ref, from_chip(o))
        for p in offsets:
            if far(p) and first_hop(p) == o:
                direct[p] = send(view, view, dev_chip(to_chip(second_hop(p)), c))
        paired[o] = send(view, view, other)

    conv_direct, conv_pair = start_gather(conv_h, W)

    def arrive(copies):
        for copy in copies:
            copy.wait_recv()

    def far_stage(buf):
        view = buf.at[pl.ds(slot, 1)]
        return [send(view, view, dev_dp(yh, lax.rem(zh + j, ZH), zl)) for j in range(1, ZH)]

    def row(buf, y):
        return buf.at[pl.ds((zl * YH + y) * ZH, ZH)]

    def y_stage(buf):
        view = row(buf, yh)
        return {
            j: send(view, view, dev_dp(lax.rem(yh + j + YH, YH), zh, zl)) for j in near(YH)
        }

    def near_stage(view):
        return [send(view, view, dev_z(j)) for j in near_z]

    part_copies = far_stage(part)

    ri = lax.broadcasted_iota(jnp.int32, (images, images * POS), 1)
    ii = lax.broadcasted_iota(jnp.int32, (images, images * POS), 0)
    pool_mat = jnp.where((ri >= ii * POS) & (ri < ii * POS + POS), 1.0, 0.0).astype(BF16)
    ri = lax.broadcasted_iota(jnp.int32, (images * POS, images), 0)
    ii = lax.broadcasted_iota(jnp.int32, (images * POS, images), 1)
    spread_mat = jnp.where((ri >= ii * POS) & (ri < ii * POS + POS), 1.0, 0.0).astype(BF16)

    def lanes(kk):
        return pl.ds(pl.multiple_of(kk * 256, 256), 256)

    def forward(kk):
        pre = dot(feat[...], W[kk], ((1,), (1,))) + short[:, lanes(kk)].astype(F32)
        h = jnp.maximum(pre, 0.0)
        hi = h.astype(BF16)
        low = (h - hi.astype(F32)).astype(BF16)
        hid[kk] = hi
        total = dot(pool_mat, hi) + dot(pool_mat, low)
        pooled[kk] = (total / POS).astype(BF16)

    for copy in local[:3]:
        copy.wait()
    proj_direct = proj_pair = None
    for n, o in enumerate(offsets):
        if n:
            landed(W, o, conv_direct, conv_pair)
            if n == 1:
                proj_direct, proj_pair = start_gather(proj_h, PW)
            last = offsets[n - 1]
            conv_pair[last].wait_recv()
            forward(from_chip(last))
        if n == min(1, chips - 1):
            featT[...] = jnp.transpose(feat[...].astype(F32)).astype(BF16)
    if chips == 1:
        proj_direct, proj_pair = start_gather(proj_h, PW)
    arrive(part_copies)
    part_copies = y_stage(part)
    for o in offsets[1:]:
        landed(PW, o, proj_direct, proj_pair)
    conv_pair[offsets[-1]].wait_recv()
    forward(from_chip(offsets[-1]))
    local[3].wait()
    arrive(part_copies.values())
    part_copies = near_stage(part.at[pl.ds(zl * YH * ZH, YH * ZH)])

    own = jnp.zeros((images, emb_w), F32)
    for o in offsets:
        proj_pair[o].wait_recv()
        kk = from_chip(o)
        own = own + dot(pooled[kk], PW[kk])

    emb[pl.ds(slot, 1)] = own[None]
    arrive(far_stage(emb))
    y_copies = y_stage(emb)
    copies = near_stage(row(emb, yh))
    for j, copy in y_copies.items():
        copy.wait_recv()
        copies += near_stage(row(emb, lax.rem(yh - j + YH, YH)))
    arrive(copies)
    arrive(part_copies)

    zall = emb[...].reshape(group, emb_w)
    center = jnp.mean(zall, axis=0, keepdims=True)
    zc = zall - center
    zbuf[...] = zc
    top = zc.astype(BF16)
    parts[:, 0:emb_w] = top
    parts[:, emb_w:] = (zc - top.astype(F32)).astype(BF16)
    sq_col = jnp.sum(zc * zc, axis=1, keepdims=True)
    spread = 2.0 * jnp.sum(sq_col) / group
    sq_wide = jnp.broadcast_to(sq_col, (group, 128))
    sqs[...] = sq_wide
    sq_row = jnp.transpose(sq_wide)[0:1]
    lane = lax.broadcasted_iota(jnp.int32, (1, group), 1)
    ls = lane // images
    lzl = ls // (YH * ZH)
    lyh = (ls // ZH) % YH
    lzh = ls % ZH
    member = (((lyh * ZH + lzh) * ZL + lzl) * images + lane % images).astype(F32)

    step = 256 if group % 256 == 0 else group
    scale = 1.0 / (2.0 * spread)

    def kernel_rows(i, carry):
        col_sum, positive = carry
        rows = pl.ds(pl.multiple_of(i * (step // images), step // images), step // images)
        at = pl.ds(pl.multiple_of(i * step, step), step)
        zt, zm = parts[at, 0:emb_w], parts[at, emb_w:]
        inner = dot(jnp.concatenate([zt, zt], axis=1), parts[...], ((1,), (1,)))
        inner = inner + dot(zm, parts[:, 0:emb_w], ((1,), (1,)))
        kk = jnp.exp(-(sqs[at, 0:1] + sq_row - 2.0 * inner) * scale)
        kmat[at, :] = kk
        rcol[at, :] = jnp.broadcast_to(jnp.mean(kk, axis=1, keepdims=True), (step, 128))
        who = part[rows].reshape(step, 128)[:, 0:1]
        positive = positive + jnp.sum(jnp.where(who == member, kk, 0.0), axis=0, keepdims=True)
        return col_sum + jnp.sum(kk, axis=0, keepdims=True), positive

    zero = jnp.zeros((1, group), F32)
    col_sum, positive = lax.fori_loop(0, group // step, kernel_rows, (zero, zero))
    row_mean = col_sum / group
    t = jnp.sum(row_mean) / group

    def square_rows(i, carry):
        at = pl.ds(pl.multiple_of(i * step, step), step)
        cen = kmat[at, :] - rcol[at, 0:1] - row_mean + t
        return carry + jnp.sum(cen * cen, axis=0, keepdims=True)

    sums = lax.fori_loop(0, group // step, square_rows, zero)
    scale_sq = float(group - 1) ** 2
    root_v = jnp.sqrt(jnp.broadcast_to(jnp.sum(sums) / scale_sq + EPSILON, (1, 128)))
    loss = -(jnp.sum(positive) / group - t) + GAMMA * root_v
    oloss[...] = loss
    root = root_v[0:1, 0:1]

    at = pl.ds(pl.multiple_of(slot * images, images), images)
    k_own = kmat[at, :]
    cen = k_own - rcol[at, 0:1] - row_mean + t
    who = part[pl.ds(slot, 1)].reshape(images, 128)[:, 0:1]
    hot = jnp.where(who == member, 1.0, 0.0)
    coeff = (-hot / group + 1.0 / (group * group) + GAMMA * cen / (scale_sq * root)) / (chips * 2)
    weighted = coeff * k_own
    z_own = zbuf[at, :]
    w_top = weighted.astype(BF16)
    w_low = (weighted - w_top.astype(F32)).astype(BF16)
    moved = dot(w_top, parts[:, 0:emb_w]) + dot(w_top, parts[:, emb_w:])
    moved = moved + dot(w_low, parts[:, 0:emb_w])
    grad = -(2.0 / spread) * (
        jnp.sum(weighted, axis=1, keepdims=True) * z_own
        - moved
    )
    ge = grad.astype(BF16)
    geT = jnp.transpose(ge.astype(F32)).astype(BF16)

    def backward(n, kk):
        gp = (dot(ge, PW[kk], ((1,), (1,))) / POS).astype(BF16)
        rows = dot(spread_mat, gp)
        gh = jnp.where(hid[kk].astype(F32) > 0.0, rows, 0.0).astype(BF16)
        conv_t = dot(featT[...], gh).astype(BF16)
        proj_t = dot(geT, pooled[kk]).astype(BF16)
        for half in range(2):
            cols = slice(half * 128, half * 128 + 128)
            term[n, half, 0:width] = conv_t[:, cols]
            term[n, half, width:] = proj_t[:, cols]

    order = [o for o in offsets if far(o)]
    order += [o for o in offsets[1:] if o[0] == 0 and o[1] in (1, X - 1)]
    order += [o for o in offsets[1:] if o not in order and o[0] == 0]
    order += [o for o in offsets[1:] if o not in order] + [offsets[0]]
    core_copies = {}
    relayed = {o: [] for o in offsets}
    group_copies = []

    def pair(n):
        o = order[n]
        core_copies[n].wait_recv()
        total = term[n, pl.ds(c, 1)][0].astype(F32) + core_in[n].astype(F32)
        for m, copy in relayed[o]:
            copy.wait_recv()
            total = total + group_in[m].astype(F32)
        pair_sum[n] = total.astype(BF16)
        if far(o):
            copy = send(pair_sum.at[n], group_in.at[n], dev_chip(to_chip(second_hop(o)), c))
            relayed[first_hop(o)].append((n, copy))
        elif n < len(order) - 1:
            copy = send(pair_sum.at[n], group_in.at[n], dev_chip(to_chip(o), c))
            group_copies.append((n, copy))

    for n, o in enumerate(order):
        backward(n, to_chip(o))
        core_copies[n] = send(term.at[n, 1 - c], core_in.at[n], other)
        if n:
            pair(n - 1)
    last = len(order) - 1
    pair(last)
    total = pair_sum[last].astype(F32)
    for n, copy in group_copies:
        copy.wait_recv()
        total = total + group_in[n].astype(F32)
    red0[...] = total.astype(BF16).reshape(red0.shape)

    copies = []
    for i, j in enumerate(near_z):
        copies.append(send(red0.at[lax.rem(zl + j + ZL, ZL)], red0_in.at[i], dev_z(j)))
    arrive(copies)
    total = red0[zl].astype(F32)
    for i in range(ZL - 1):
        total = total + red0_in[i].astype(F32)
    red1[...] = total.astype(BF16)
    copies = []
    for j in range(1, ZH):
        q = lax.rem(zh + j, ZH)
        copies.append(send(red1.at[q], red1_in.at[j], dev_dp(yh, q, zl)))
    arrive(copies)
    total = red1[zh].astype(F32)
    for j in range(1, ZH):
        total = total + red1_in[j].astype(F32)
    red2[yh] = total.astype(BF16)
    copies = []
    for j in range(1, YH):
        q = lax.rem(yh + j, YH)
        copies.append(send(red2.at[yh], red2.at[yh], dev_dp(q, zh, zl)))
    arrive(copies)
    total = red2[0].astype(F32)
    for j in range(1, YH):
        total = total + red2[j].astype(F32)
    fin[zl, zh] = total.astype(BF16)
    copies = []
    for j in range(1, ZH):
        q = lax.rem(zh + j, ZH)
        copies.append(send(fin.at[zl, zh], fin.at[zl, zh], dev_dp(yh, q, zl)))
    arrive(copies)
    copies = []
    for j in near_z:
        copies.append(send(fin.at[zl], fin.at[zl], dev_z(j)))
    arrive(copies)

    result = fin[...].astype(F32).reshape(width + emb_w, 128)
    oconv[...] = jnp.transpose(result[0:width])
    oproj[...] = jnp.transpose(result[width:])

    for copy in pending:
        copy.wait_send()


def local(features, shortcut, conv_weight, proj_weight, partner):
    rows, width = features.shape
    emb_w = proj_weight.shape[1]
    chips = YL * X
    dp = YH * ZH * ZL
    group = dp * 8
    both = width + emb_w
    piece = both // (ZL * ZH)
    sends = 100
    hbm = pl.BlockSpec(memory_space=pltpu.HBM)
    vmem = pl.BlockSpec(memory_space=pltpu.VMEM)
    grad_conv, grad_proj, loss = pl.pallas_call(
        kernel,
        out_shape=(
            jax.ShapeDtypeStruct((128, width), F32),
            jax.ShapeDtypeStruct((128, emb_w), F32),
            jax.ShapeDtypeStruct((1, 128), F32),
        ),
        in_specs=[hbm, hbm, hbm, hbm, pl.BlockSpec(memory_space=pltpu.SMEM)],
        out_specs=(vmem, vmem, vmem),
        scratch_shapes=[
            pltpu.VMEM((rows, width), BF16),
            pltpu.VMEM((rows, chips * 256), BF16),
            pltpu.VMEM((width, rows), BF16),
            pltpu.VMEM((chips, 256, width), BF16),
            pltpu.VMEM((chips, 256, emb_w), BF16),
            pltpu.VMEM((chips, rows, 256), BF16),
            pltpu.VMEM((chips, 8, 256), BF16),
            pltpu.VMEM((dp, 8, 128), F32),
            pltpu.VMEM((dp, 8, emb_w), F32),
            pltpu.VMEM((group, emb_w), F32),
            pltpu.VMEM((group, 2 * emb_w), BF16),
            pltpu.VMEM((group, 128), F32),
            pltpu.VMEM((group, group), F32),
            pltpu.VMEM((group, 128), F32),
            pltpu.VMEM((chips, 2, both, 128), BF16),
            pltpu.VMEM((chips, both, 128), BF16),
            pltpu.VMEM((chips, both, 128), BF16),
            pltpu.VMEM((chips, both, 128), BF16),
            pltpu.VMEM((ZL, ZH, piece, 128), BF16),
            pltpu.VMEM((ZL, ZH, piece, 128), BF16),
            pltpu.VMEM((ZH, piece, 128), BF16),
            pltpu.VMEM((ZH, piece, 128), BF16),
            pltpu.VMEM((YH, piece, 128), BF16),
            pltpu.VMEM((ZL, ZH, piece, 128), BF16),
            pltpu.SemaphoreType.DMA((4,)),
            pltpu.SemaphoreType.DMA((sends,)),
            pltpu.SemaphoreType.DMA((sends,)),
        ],
        compiler_params=pltpu.CompilerParams(
            collective_id=0, has_side_effects=True, vmem_limit_bytes=63 << 20
        ),
    )(features, shortcut, conv_weight, proj_weight, partner)
    return grad_conv, grad_proj, loss[0, 0:1]


def solution(mesh):
    return jax.shard_map(
        local,
        mesh=mesh,
        in_specs=(
            P(("dp", "fsdp"), None),
            P(("dp", "fsdp"), None),
            P("fsdp", None),
            P("fsdp", None),
            P(("dp", "fsdp")),
        ),
        out_specs=(P("fsdp", None), P("fsdp", None), P("fsdp")),
        check_vma=False,
    )
```

```python
import jax
import jax.numpy as jnp
from jax import lax
from jax.experimental import pallas as pl
from jax.experimental.pallas import tpu as pltpu
from jax.sharding import PartitionSpec as P

MESH = pl.DeviceIdType.MESH
BF16 = jnp.bfloat16
F32 = jnp.float32

POS = 49
GAMMA = 3.0
EPSILON = 1e-06

YH, ZH, ZL = 4, 4, 4
YL, X = 2, 4


def far(o):
    return o[0] > 0 and o[1] > 0


def first_hop(o):
    return (o[0], 0) if o[1] in (1, X - 1) else (0, o[1])


def second_hop(o):
    return (0, o[1]) if o[1] in (1, X - 1) else (o[0], 0)


def z_plan(n):
    if n == 16:
        return [1, -1, 2, -2], 5, 13
    return near(n), 0, 1


def near(n):
    return [j if j <= n // 2 else j - n for j in sorted(range(1, n), key=lambda j: min(j, n - j))]


def dot(a, b, dims=((1,), (0,)), precision=None):
    return lax.dot_general(
        a, b, (dims, ((), ())), precision=precision, preferred_element_type=F32
    )


def kernel(
    feat_h, short_h, conv_h, proj_h, partner_h,
    oconv, oproj, oloss,
    feat, short, featT, W, PW, hid, pooled, part, emb, zbuf, parts, sqs, kmat, rcol,
    term, core_in, pair_sum, group_in,
    red0, close_in, red1, reach_in, opp_in, red2, done, close_done, opp_done, fin,
    partner_s, lsem, ssem, rsem,
):
    chips = YL * X
    dp = YH * ZH * ZL
    images = 8
    width = feat.shape[1]
    emb_w = emb.shape[2]
    group = dp * images

    d = lax.axis_index("dp")
    f = lax.axis_index("fsdp")
    yh = lax.div(d, ZH * ZL)
    zh = lax.rem(lax.div(d, ZL), ZH)
    zl = lax.rem(d, ZL)
    chip = lax.div(f, 2)
    yl = lax.div(chip, X)
    x = lax.rem(chip, X)
    c = lax.rem(f, 2)

    def dev_chip(ch, core):
        return (d, ch * 2 + core)

    def dev_dp(a, b, e):
        return ((a * ZH + b) * ZL + e, f)

    used = [0]
    pending = []

    def send(src, dst, dev):
        i = used[0]
        used[0] += 1
        copy = pltpu.make_async_remote_copy(
            src_ref=src, dst_ref=dst, send_sem=ssem.at[i], recv_sem=rsem.at[i],
            device_id=dev, device_id_type=MESH,
        )
        copy.start()
        pending.append(copy)
        return copy

    offsets = [(dy, dx) for dy in range(YL) for dx in range(X)]
    offsets.sort(key=lambda o: (far(o), o[0] + min(o[1], X - o[1]), -o[0]))

    def to_chip(o):
        return lax.rem(yl + o[0], YL) * X + lax.rem(x + o[1], X)

    def from_chip(o):
        return lax.rem(yl + YL - o[0], YL) * X + lax.rem(x + X - o[1], X)

    mine = pl.ds(pl.multiple_of(c * 128, 128), 128)
    local = [
        pltpu.make_async_copy(conv_h, W.at[chip, mine], lsem.at[0]),
        pltpu.make_async_copy(feat_h, feat, lsem.at[1]),
        pltpu.make_async_copy(short_h, short, lsem.at[2]),
        pltpu.make_async_copy(proj_h, PW.at[chip, mine], lsem.at[3]),
        pltpu.make_async_copy(partner_h, partner_s, lsem.at[4]),
    ]
    for copy in local:
        copy.start()

    peers = [dev_chip(chip, 1 - c)]
    peers += [dev_chip(to_chip(o), c) for o in offsets[1:] if not far(o)]
    peers += [dev_dp(lax.rem(yh + j, YH), zh, zl) for j in range(1, YH)]
    Z = ZH * ZL
    z = zh * ZL + zl

    def zmod(j):
        return lax.rem(z + j + Z, Z)

    def dev_z(j):
        return (yh * Z + zmod(j), f)

    near_z = near(ZL)
    close, reach, inverse = z_plan(Z)
    steps = near_z + close + [j * ZL for j in range(1, ZH)] + ([reach, 8] if reach else [])
    steps = {j % Z for j in steps} | {-j % Z for j in steps}
    peers += [dev_z(j) for j in sorted(steps)]
    barrier = pltpu.get_barrier_semaphore()
    for peer in peers:
        pl.semaphore_signal(barrier, inc=1, device_id=peer, device_id_type=MESH)

    slot = (zl * YH + yh) * ZH + zh
    row8 = lax.broadcasted_iota(jnp.int32, (images, 128), 0)
    local[4].wait()
    column = jnp.zeros((images, 128), jnp.int32)
    for i in range(images):
        column = jnp.where(row8 == i, partner_s[i], column)
    part[pl.ds(slot, 1)] = column.astype(F32)[None]

    pl.semaphore_wait(barrier, len(peers))

    other = dev_chip(chip, 1 - c)

    def block(ref, ch):
        return ref.at[ch, mine]

    def start_gather(source, ref):
        direct = {}
        for o in offsets[1:]:
            if not far(o):
                direct[o] = send(source, block(ref, chip), dev_chip(to_chip(o), c))
        return direct, {offsets[0]: send(source, block(ref, chip), other)}

    def landed(ref, o, direct, paired):
        direct[o].wait_recv()
        view = block(ref, from_chip(o))
        for p in offsets:
            if far(p) and first_hop(p) == o:
                direct[p] = send(view, view, dev_chip(to_chip(second_hop(p)), c))
        paired[o] = send(view, view, other)

    conv_direct, conv_pair = start_gather(conv_h, W)

    def arrive(copies):
        for copy in copies:
            copy.wait_recv()

    def far_stage(buf):
        view = buf.at[pl.ds(slot, 1)]
        return [send(view, view, dev_dp(yh, lax.rem(zh + j, ZH), zl)) for j in range(1, ZH)]

    def row(buf, y):
        return buf.at[pl.ds((zl * YH + y) * ZH, ZH)]

    def y_stage(buf):
        view = row(buf, yh)
        return {
            j: send(view, view, dev_dp(lax.rem(yh + j + YH, YH), zh, zl)) for j in near(YH)
        }

    def near_stage(view):
        return [send(view, view, dev_z(j)) for j in near_z]

    part_copies = far_stage(part)

    ri = lax.broadcasted_iota(jnp.int32, (images, images * POS), 1)
    ii = lax.broadcasted_iota(jnp.int32, (images, images * POS), 0)
    pool_mat = jnp.where((ri >= ii * POS) & (ri < ii * POS + POS), 1.0, 0.0).astype(BF16)
    ri = lax.broadcasted_iota(jnp.int32, (images * POS, images), 0)
    ii = lax.broadcasted_iota(jnp.int32, (images * POS, images), 1)
    spread_mat = jnp.where((ri >= ii * POS) & (ri < ii * POS + POS), 1.0, 0.0).astype(BF16)

    def lanes(kk):
        return pl.ds(pl.multiple_of(kk * 256, 256), 256)

    def forward(kk):
        pre = dot(feat[...], W[kk], ((1,), (1,))) + short[:, lanes(kk)].astype(F32)
        h = jnp.maximum(pre, 0.0)
        hi = h.astype(BF16)
        low = (h - hi.astype(F32)).astype(BF16)
        hid[kk] = hi
        total = dot(pool_mat, hi) + dot(pool_mat, low)
        pooled[kk] = (total / POS).astype(BF16)

    for copy in local[:3]:
        copy.wait()
    proj_direct = proj_pair = None
    for n, o in enumerate(offsets):
        if n:
            landed(W, o, conv_direct, conv_pair)
            if n == 1:
                proj_direct, proj_pair = start_gather(proj_h, PW)
            last = offsets[n - 1]
            conv_pair[last].wait_recv()
            forward(from_chip(last))
        if n == min(1, chips - 1):
            featT[...] = jnp.transpose(feat[...].astype(F32)).astype(BF16)
    if chips == 1:
        proj_direct, proj_pair = start_gather(proj_h, PW)
    arrive(part_copies)
    part_copies = y_stage(part)
    for o in offsets[1:]:
        landed(PW, o, proj_direct, proj_pair)
    conv_pair[offsets[-1]].wait_recv()
    forward(from_chip(offsets[-1]))
    local[3].wait()
    arrive(part_copies.values())
    part_copies = near_stage(part.at[pl.ds(zl * YH * ZH, YH * ZH)])

    own = jnp.zeros((images, emb_w), F32)
    for o in offsets:
        proj_pair[o].wait_recv()
        kk = from_chip(o)
        own = own + dot(pooled[kk], PW[kk])

    emb[pl.ds(slot, 1)] = own[None]
    arrive(far_stage(emb))
    y_copies = y_stage(emb)
    copies = near_stage(row(emb, yh))
    for j, copy in y_copies.items():
        copy.wait_recv()
        copies += near_stage(row(emb, lax.rem(yh - j + YH, YH)))
    arrive(copies)
    arrive(part_copies)

    zall = emb[...].reshape(group, emb_w)
    center = jnp.mean(zall, axis=0, keepdims=True)
    zc = zall - center
    zbuf[...] = zc
    top = zc.astype(BF16)
    parts[:, 0:emb_w] = top
    parts[:, emb_w:] = (zc - top.astype(F32)).astype(BF16)
    sq_col = jnp.sum(zc * zc, axis=1, keepdims=True)
    spread = 2.0 * jnp.sum(sq_col) / group
    sq_wide = jnp.broadcast_to(sq_col, (group, 128))
    sqs[...] = sq_wide
    sq_row = jnp.transpose(sq_wide)[0:1]
    lane = lax.broadcasted_iota(jnp.int32, (1, group), 1)
    ls = lane // images
    lzl = ls // (YH * ZH)
    lyh = (ls // ZH) % YH
    lzh = ls % ZH
    member = (((lyh * ZH + lzh) * ZL + lzl) * images + lane % images).astype(F32)

    step = 256 if group % 256 == 0 else group
    scale = 1.0 / (2.0 * spread)

    def kernel_rows(i, carry):
        col_sum, positive = carry
        rows = pl.ds(pl.multiple_of(i * (step // images), step // images), step // images)
        at = pl.ds(pl.multiple_of(i * step, step), step)
        zt, zm = parts[at, 0:emb_w], parts[at, emb_w:]
        inner = dot(jnp.concatenate([zt, zt], axis=1), parts[...], ((1,), (1,)))
        inner = inner + dot(zm, parts[:, 0:emb_w], ((1,), (1,)))
        kk = jnp.exp(-(sqs[at, 0:1] + sq_row - 2.0 * inner) * scale)
        kmat[at, :] = kk
        rcol[at, :] = jnp.broadcast_to(jnp.mean(kk, axis=1, keepdims=True), (step, 128))
        who = part[rows].reshape(step, 128)[:, 0:1]
        positive = positive + jnp.sum(jnp.where(who == member, kk, 0.0), axis=0, keepdims=True)
        return col_sum + jnp.sum(kk, axis=0, keepdims=True), positive

    zero = jnp.zeros((1, group), F32)
    col_sum, positive = lax.fori_loop(0, group // step, kernel_rows, (zero, zero))
    row_mean = col_sum / group
    t = jnp.sum(row_mean) / group

    def square_rows(i, carry):
        at = pl.ds(pl.multiple_of(i * step, step), step)
        cen = kmat[at, :] - rcol[at, 0:1] - row_mean + t
        return carry + jnp.sum(cen * cen, axis=0, keepdims=True)

    sums = lax.fori_loop(0, group // step, square_rows, zero)
    scale_sq = float(group - 1) ** 2
    root_v = jnp.sqrt(jnp.broadcast_to(jnp.sum(sums) / scale_sq + EPSILON, (1, 128)))
    loss = -(jnp.sum(positive) / group - t) + GAMMA * root_v
    oloss[...] = loss
    root = root_v[0:1, 0:1]

    at = pl.ds(pl.multiple_of(slot * images, images), images)
    k_own = kmat[at, :]
    cen = k_own - rcol[at, 0:1] - row_mean + t
    who = part[pl.ds(slot, 1)].reshape(images, 128)[:, 0:1]
    hot = jnp.where(who == member, 1.0, 0.0)
    coeff = (-hot / group + 1.0 / (group * group) + GAMMA * cen / (scale_sq * root)) / (chips * 2)
    weighted = coeff * k_own
    z_own = zbuf[at, :]
    w_top = weighted.astype(BF16)
    w_low = (weighted - w_top.astype(F32)).astype(BF16)
    moved = dot(w_top, parts[:, 0:emb_w]) + dot(w_top, parts[:, emb_w:])
    moved = moved + dot(w_low, parts[:, 0:emb_w])
    grad = -(2.0 / spread) * (
        jnp.sum(weighted, axis=1, keepdims=True) * z_own
        - moved
    )
    ge = grad.astype(BF16)
    geT = jnp.transpose(ge.astype(F32)).astype(BF16)

    def backward(n, kk):
        gp = (dot(ge, PW[kk], ((1,), (1,))) / POS).astype(BF16)
        rows = dot(spread_mat, gp)
        gh = jnp.where(hid[kk].astype(F32) > 0.0, rows, 0.0).astype(BF16)
        conv_t = dot(featT[...], gh).astype(BF16)
        proj_t = dot(geT, pooled[kk]).astype(BF16)
        for half in range(2):
            cols = slice(half * 128, half * 128 + 128)
            term[n, half, 0:width] = conv_t[:, cols]
            term[n, half, width:] = proj_t[:, cols]

    order = [o for o in offsets if far(o)]
    order += [o for o in offsets[1:] if o[0] == 0 and o[1] in (1, X - 1)]
    order += [o for o in offsets[1:] if o not in order and o[0] == 0]
    order += [o for o in offsets[1:] if o not in order] + [offsets[0]]
    core_copies = {}
    relayed = {o: [] for o in offsets}
    group_copies = []

    def pair(n):
        o = order[n]
        core_copies[n].wait_recv()
        total = term[n, pl.ds(c, 1)][0].astype(F32) + core_in[n].astype(F32)
        for m, copy in relayed[o]:
            copy.wait_recv()
            total = total + group_in[m].astype(F32)
        pair_sum[n] = total.astype(BF16)
        if far(o):
            copy = send(pair_sum.at[n], group_in.at[n], dev_chip(to_chip(second_hop(o)), c))
            relayed[first_hop(o)].append((n, copy))
        elif n < len(order) - 1:
            copy = send(pair_sum.at[n], group_in.at[n], dev_chip(to_chip(o), c))
            group_copies.append((n, copy))

    for n, o in enumerate(order):
        backward(n, to_chip(o))
        core_copies[n] = send(term.at[n, 1 - c], core_in.at[n], other)
        if n:
            pair(n - 1)
    last = len(order) - 1
    pair(last)
    total = pair_sum[last].astype(F32)
    for n, copy in group_copies:
        copy.wait_recv()
        total = total + group_in[n].astype(F32)
    total = total.astype(BF16)
    span = 3 if reach else 1
    mid = span // 2
    piece = red0.shape[1]
    for p in range(Z + span - 1):
        q = (reach * p) % Z if reach else p
        red0[p] = total[q * piece : (q + 1) * piece]

    def position(j):
        return lax.rem(inverse * zmod(j) + Z - mid, Z)

    copies = []
    for i, j in enumerate(close):
        copies.append(send(red0.at[pl.ds(position(j), span)], close_in.at[i], dev_z(j)))
    if reach:
        opposite = send(red0.at[lax.rem(inverse * zmod(8), Z)], opp_in, dev_z(8))
    arrive(copies)
    total = red0[pl.ds(position(0), span)].astype(F32)
    for i in range(len(close)):
        total = total + close_in[i].astype(F32)
    if reach:
        red1[...] = total.astype(BF16)
        copies = [
            send(red1.at[0], reach_in.at[0], dev_z(-reach)),
            send(red1.at[2], reach_in.at[1], dev_z(reach)),
        ]
        opposite.wait_recv()
        total = total[mid] + opp_in[...].astype(F32)
        arrive(copies)
        total = total + reach_in[0].astype(F32) + reach_in[1].astype(F32)
    else:
        total = total[mid]
    red2[yh] = total.astype(BF16)
    copies = []
    for j in range(1, YH):
        q = lax.rem(yh + j, YH)
        copies.append(send(red2.at[yh], red2.at[yh], dev_dp(q, zh, zl)))
    arrive(copies)
    total = red2[0].astype(F32)
    for j in range(1, YH):
        total = total + red2[j].astype(F32)
    done[mid] = total.astype(BF16)
    if reach:
        copies = [
            send(done.at[1], done.at[0], dev_z(reach)),
            send(done.at[1], done.at[2], dev_z(-reach)),
        ]
        opposite = send(done.at[1], opp_done, dev_z(8))
        arrive(copies)
    copies = [send(done, close_done.at[i], dev_z(j)) for i, j in enumerate(close)]
    for k in range(span):
        fin[zmod(reach * (k - mid))] = done[k]
    if reach:
        opposite.wait_recv()
        fin[zmod(8)] = opp_done[...]
    for i, j in enumerate(close):
        copies[i].wait_recv()
        for k in range(span):
            fin[zmod(reach * (k - mid) - j)] = close_done[i, k]

    result = fin[...].astype(F32).reshape(width + emb_w, 128)
    oconv[...] = jnp.transpose(result[0:width])
    oproj[...] = jnp.transpose(result[width:])

    for copy in pending:
        copy.wait_send()


def local(features, shortcut, conv_weight, proj_weight, partner):
    rows, width = features.shape
    emb_w = proj_weight.shape[1]
    chips = YL * X
    dp = YH * ZH * ZL
    group = dp * 8
    both = width + emb_w
    Z = ZL * ZH
    piece = both // Z
    close, reach, _ = z_plan(Z)
    span = 3 if reach else 1
    sends = 100
    hbm = pl.BlockSpec(memory_space=pltpu.HBM)
    args = (features, shortcut, conv_weight, proj_weight, partner)
    args = [pltpu.with_memory_space_constraint(arg, pltpu.HBM) for arg in args]
    vmem = pl.BlockSpec(memory_space=pltpu.VMEM)
    grad_conv, grad_proj, loss = pl.pallas_call(
        kernel,
        out_shape=(
            jax.ShapeDtypeStruct((128, width), F32),
            jax.ShapeDtypeStruct((128, emb_w), F32),
            jax.ShapeDtypeStruct((1, 128), F32),
        ),
        in_specs=[hbm] * 5,
        out_specs=(vmem, vmem, vmem),
        scratch_shapes=[
            pltpu.VMEM((rows, width), BF16),
            pltpu.VMEM((rows, chips * 256), BF16),
            pltpu.VMEM((width, rows), BF16),
            pltpu.VMEM((chips, 256, width), BF16),
            pltpu.VMEM((chips, 256, emb_w), BF16),
            pltpu.VMEM((chips, rows, 256), BF16),
            pltpu.VMEM((chips, 8, 256), BF16),
            pltpu.VMEM((dp, 8, 128), F32),
            pltpu.VMEM((dp, 8, emb_w), F32),
            pltpu.VMEM((group, emb_w), F32),
            pltpu.VMEM((group, 2 * emb_w), BF16),
            pltpu.VMEM((group, 128), F32),
            pltpu.VMEM((group, group), F32),
            pltpu.VMEM((group, 128), F32),
            pltpu.VMEM((chips, 2, both, 128), BF16),
            pltpu.VMEM((chips, both, 128), BF16),
            pltpu.VMEM((chips, both, 128), BF16),
            pltpu.VMEM((chips, both, 128), BF16),
            pltpu.VMEM((Z + span - 1, piece, 128), BF16),
            pltpu.VMEM((len(close) or 1, span, piece, 128), BF16),
            pltpu.VMEM((span, piece, 128), BF16),
            pltpu.VMEM((2, piece, 128), BF16),
            pltpu.VMEM((piece, 128), BF16),
            pltpu.VMEM((YH, piece, 128), BF16),
            pltpu.VMEM((span, piece, 128), BF16),
            pltpu.VMEM((len(close) or 1, span, piece, 128), BF16),
            pltpu.VMEM((piece, 128), BF16),
            pltpu.VMEM((Z, piece, 128), BF16),
            pltpu.SMEM((8,), jnp.int32),
            pltpu.SemaphoreType.DMA((5,)),
            pltpu.SemaphoreType.DMA((sends,)),
            pltpu.SemaphoreType.DMA((sends,)),
        ],
        compiler_params=pltpu.CompilerParams(
            collective_id=0, has_side_effects=True, vmem_limit_bytes=48 << 20
        ),
    )(*args)
    return grad_conv, grad_proj, loss[0, 0:1]


def solution(mesh):
    return jax.shard_map(
        local,
        mesh=mesh,
        in_specs=(
            P(("dp", "fsdp"), None),
            P(("dp", "fsdp"), None),
            P("fsdp", None),
            P("fsdp", None),
            P(("dp", "fsdp")),
        ),
        out_specs=(P("fsdp", None), P("fsdp", None), P("fsdp")),
        check_vma=False,
    )
```

```python
import jax
import jax.numpy as jnp
from jax import lax
from jax.experimental import pallas as pl
from jax.experimental.pallas import tpu as pltpu
from jax.sharding import PartitionSpec as P

MESH = pl.DeviceIdType.MESH
BF16 = jnp.bfloat16
F32 = jnp.float32

POS = 49
GAMMA = 3.0
EPSILON = 1e-06

YH, ZH, ZL = 4, 4, 4
YL, X = 2, 4


def far(o):
    return o[0] > 0 and o[1] > 0


def first_hop(o):
    return (o[0], 0) if o[1] in (1, X - 1) else (0, o[1])


def second_hop(o):
    return (0, o[1]) if o[1] in (1, X - 1) else (o[0], 0)


def z_plan(n):
    if n == 16:
        return [1, -1, 2, -2], 5, 13
    return near(n), 0, 1


def near(n):
    return [j if j <= n // 2 else j - n for j in sorted(range(1, n), key=lambda j: min(j, n - j))]


def dot(a, b, dims=((1,), (0,)), precision=None):
    return lax.dot_general(
        a, b, (dims, ((), ())), precision=precision, preferred_element_type=F32
    )


def kernel(
    feat_h, short_h, conv_h, proj_h, partner_h,
    oconv, oproj, oloss,
    feat, short, featT, W, PW, hid, pooled, part, emb, zbuf, parts, sqs, kmat, rcol,
    term, core_in, pair_sum, group_in,
    red0, close_in, red1, reach_in, opp_in, red2, done, close_done, opp_done, fin,
    partner_s, lsem, ssem, rsem,
):
    chips = YL * X
    dp = YH * ZH * ZL
    images = 8
    width = feat.shape[1]
    emb_w = emb.shape[2]
    group = dp * images

    d = lax.axis_index("dp")
    f = lax.axis_index("fsdp")
    yh = lax.div(d, ZH * ZL)
    zh = lax.rem(lax.div(d, ZL), ZH)
    zl = lax.rem(d, ZL)
    chip = lax.div(f, 2)
    yl = lax.div(chip, X)
    x = lax.rem(chip, X)
    c = lax.rem(f, 2)

    def dev_chip(ch, core):
        return (d, ch * 2 + core)

    def dev_dp(a, b, e):
        return ((a * ZH + b) * ZL + e, f)

    used = [0]
    pending = []

    def send(src, dst, dev):
        i = used[0]
        used[0] += 1
        copy = pltpu.make_async_remote_copy(
            src_ref=src, dst_ref=dst, send_sem=ssem.at[i], recv_sem=rsem.at[i],
            device_id=dev, device_id_type=MESH,
        )
        copy.start()
        pending.append(copy)
        return copy

    def sent(n):
        for copy in pending[:n]:
            copy.wait_send()
        del pending[:n]

    offsets = [(dy, dx) for dy in range(YL) for dx in range(X)]
    offsets.sort(key=lambda o: (far(o), o[0] + min(o[1], X - o[1]), -o[0]))

    def to_chip(o):
        return lax.rem(yl + o[0], YL) * X + lax.rem(x + o[1], X)

    def from_chip(o):
        return lax.rem(yl + YL - o[0], YL) * X + lax.rem(x + X - o[1], X)

    mine = pl.ds(pl.multiple_of(c * 128, 128), 128)
    local = [
        pltpu.make_async_copy(conv_h, W.at[chip, mine], lsem.at[0]),
        pltpu.make_async_copy(feat_h, feat, lsem.at[1]),
        pltpu.make_async_copy(short_h, short, lsem.at[2]),
        pltpu.make_async_copy(proj_h, PW.at[chip, mine], lsem.at[3]),
        pltpu.make_async_copy(partner_h, partner_s, lsem.at[4]),
    ]
    for copy in local:
        copy.start()

    peers = [dev_chip(chip, 1 - c)]
    peers += [dev_chip(to_chip(o), c) for o in offsets[1:] if not far(o)]
    peers += [dev_dp(lax.rem(yh + j, YH), zh, zl) for j in range(1, YH)]
    Z = ZH * ZL
    z = zh * ZL + zl

    def zmod(j):
        return lax.rem(z + j + Z, Z)

    def dev_z(j):
        return (yh * Z + zmod(j), f)

    near_z = near(ZL)
    close, reach, inverse = z_plan(Z)
    steps = near_z + close + [j * ZL for j in range(1, ZH)] + ([reach, 8] if reach else [])
    steps = {j % Z for j in steps} | {-j % Z for j in steps}
    peers += [dev_z(j) for j in sorted(steps)]
    barrier = pltpu.get_barrier_semaphore()
    for peer in peers:
        pl.semaphore_signal(barrier, inc=1, device_id=peer, device_id_type=MESH)

    slot = (zl * YH + yh) * ZH + zh
    row8 = lax.broadcasted_iota(jnp.int32, (images, 128), 0)
    local[4].wait()
    column = jnp.zeros((images, 128), jnp.int32)
    for i in range(images):
        column = jnp.where(row8 == i, partner_s[i], column)
    part[pl.ds(slot, 1)] = column.astype(F32)[None]

    pl.semaphore_wait(barrier, len(peers))

    other = dev_chip(chip, 1 - c)

    def block(ref, ch):
        return ref.at[ch, mine]

    def start_gather(source, ref):
        direct = {}
        for o in offsets[1:]:
            if not far(o):
                direct[o] = send(source, block(ref, chip), dev_chip(to_chip(o), c))
        return direct, {offsets[0]: send(source, block(ref, chip), other)}

    def landed(ref, o, direct, paired):
        direct[o].wait_recv()
        view = block(ref, from_chip(o))
        for p in offsets:
            if far(p) and first_hop(p) == o:
                direct[p] = send(view, view, dev_chip(to_chip(second_hop(p)), c))
        paired[o] = send(view, view, other)

    conv_direct, conv_pair = start_gather(conv_h, W)

    def arrive(copies):
        for copy in copies:
            copy.wait_recv()

    def far_stage(buf):
        view = buf.at[pl.ds(slot, 1)]
        return [send(view, view, dev_dp(yh, lax.rem(zh + j, ZH), zl)) for j in range(1, ZH)]

    def row(buf, y):
        return buf.at[pl.ds((zl * YH + y) * ZH, ZH)]

    def y_stage(buf):
        view = row(buf, yh)
        return {
            j: send(view, view, dev_dp(lax.rem(yh + j + YH, YH), zh, zl)) for j in near(YH)
        }

    def near_stage(view):
        return [send(view, view, dev_z(j)) for j in near_z]

    part_copies = far_stage(part)

    ri = lax.broadcasted_iota(jnp.int32, (images, images * POS), 1)
    ii = lax.broadcasted_iota(jnp.int32, (images, images * POS), 0)
    pool_mat = jnp.where((ri >= ii * POS) & (ri < ii * POS + POS), 1.0, 0.0).astype(BF16)
    ri = lax.broadcasted_iota(jnp.int32, (images * POS, images), 0)
    ii = lax.broadcasted_iota(jnp.int32, (images * POS, images), 1)
    spread_mat = jnp.where((ri >= ii * POS) & (ri < ii * POS + POS), 1.0, 0.0).astype(BF16)

    def lanes(kk):
        return pl.ds(pl.multiple_of(kk * 256, 256), 256)

    def forward(kk):
        pre = dot(feat[...], W[kk], ((1,), (1,))) + short[:, lanes(kk)].astype(F32)
        h = jnp.maximum(pre, 0.0)
        hi = h.astype(BF16)
        low = (h - hi.astype(F32)).astype(BF16)
        hid[kk] = hi
        total = dot(pool_mat, hi) + dot(pool_mat, low)
        pooled[kk] = (total / POS).astype(BF16)

    for copy in local[:3]:
        copy.wait()
    proj_direct = proj_pair = None
    for n, o in enumerate(offsets):
        if n:
            landed(W, o, conv_direct, conv_pair)
            if n == 1:
                proj_direct, proj_pair = start_gather(proj_h, PW)
            last = offsets[n - 1]
            conv_pair[last].wait_recv()
            forward(from_chip(last))
        if n == min(1, chips - 1):
            featT[...] = jnp.transpose(feat[...].astype(F32)).astype(BF16)
    if chips == 1:
        proj_direct, proj_pair = start_gather(proj_h, PW)
    arrive(part_copies)
    part_copies = y_stage(part)
    for o in offsets[1:]:
        landed(PW, o, proj_direct, proj_pair)
    conv_pair[offsets[-1]].wait_recv()
    forward(from_chip(offsets[-1]))
    local[3].wait()
    arrive(part_copies.values())
    part_copies = near_stage(part.at[pl.ds(zl * YH * ZH, YH * ZH)])

    own = jnp.zeros((images, emb_w), F32)
    for o in offsets:
        proj_pair[o].wait_recv()
        kk = from_chip(o)
        own = own + dot(pooled[kk], PW[kk])

    emb[pl.ds(slot, 1)] = own[None]
    def to_y(zq):
        view = emb.at[pl.ds((zl * YH + yh) * ZH + zq, 1)]
        for j in near(YH):
            y_copies[j].append(send(view, view, dev_dp(lax.rem(yh + j + YH, YH), zh, zl)))

    y_copies = {j: [] for j in near(YH)}
    older = len(pending)
    far_copies = dict(zip(range(1, ZH), far_stage(emb)))
    to_y(zh)
    sent(older)
    for j in near(ZH):
        far_copies[j % ZH].wait_recv()
        to_y(lax.rem(zh - j + ZH, ZH))
    copies = near_stage(row(emb, yh))
    for j, landed_y in y_copies.items():
        arrive(landed_y)
        copies += near_stage(row(emb, lax.rem(yh - j + YH, YH)))
    arrive(copies)
    arrive(part_copies)

    zall = emb[...].reshape(group, emb_w)
    center = jnp.mean(zall, axis=0, keepdims=True)
    zc = zall - center
    zbuf[...] = zc
    top = zc.astype(BF16)
    parts[:, 0:emb_w] = top
    parts[:, emb_w:] = (zc - top.astype(F32)).astype(BF16)
    sq_col = jnp.sum(zc * zc, axis=1, keepdims=True)
    spread = 2.0 * jnp.sum(sq_col) / group
    sq_wide = jnp.broadcast_to(sq_col, (group, 128))
    sqs[...] = sq_wide
    sq_row = jnp.transpose(sq_wide)[0:1]
    lane = lax.broadcasted_iota(jnp.int32, (1, group), 1)
    ls = lane // images
    lzl = ls // (YH * ZH)
    lyh = (ls // ZH) % YH
    lzh = ls % ZH
    member = (((lyh * ZH + lzh) * ZL + lzl) * images + lane % images).astype(F32)

    step = 256 if group % 256 == 0 else group
    scale = 1.0 / (2.0 * spread)

    def kernel_rows(i, carry):
        col_sum, positive = carry
        rows = pl.ds(pl.multiple_of(i * (step // images), step // images), step // images)
        at = pl.ds(pl.multiple_of(i * step, step), step)
        zt, zm = parts[at, 0:emb_w], parts[at, emb_w:]
        inner = dot(jnp.concatenate([zt, zt], axis=1), parts[...], ((1,), (1,)))
        inner = inner + dot(zm, parts[:, 0:emb_w], ((1,), (1,)))
        kk = jnp.exp(-(sqs[at, 0:1] + sq_row - 2.0 * inner) * scale)
        kmat[at, :] = kk
        rcol[at, :] = jnp.broadcast_to(jnp.mean(kk, axis=1, keepdims=True), (step, 128))
        who = part[rows].reshape(step, 128)[:, 0:1]
        positive = positive + jnp.sum(jnp.where(who == member, kk, 0.0), axis=0, keepdims=True)
        return col_sum + jnp.sum(kk, axis=0, keepdims=True), positive

    zero = jnp.zeros((1, group), F32)
    col_sum, positive = lax.fori_loop(0, group // step, kernel_rows, (zero, zero))
    row_mean = col_sum / group
    t = jnp.sum(row_mean) / group

    def square_rows(i, carry):
        at = pl.ds(pl.multiple_of(i * step, step), step)
        cen = kmat[at, :] - rcol[at, 0:1] - row_mean + t
        return carry + jnp.sum(cen * cen, axis=0, keepdims=True)

    sums = lax.fori_loop(0, group // step, square_rows, zero)
    scale_sq = float(group - 1) ** 2
    root_v = jnp.sqrt(jnp.broadcast_to(jnp.sum(sums) / scale_sq + EPSILON, (1, 128)))
    loss = -(jnp.sum(positive) / group - t) + GAMMA * root_v
    oloss[...] = loss
    root = root_v[0:1, 0:1]

    at = pl.ds(pl.multiple_of(slot * images, images), images)
    k_own = kmat[at, :]
    cen = k_own - rcol[at, 0:1] - row_mean + t
    who = part[pl.ds(slot, 1)].reshape(images, 128)[:, 0:1]
    hot = jnp.where(who == member, 1.0, 0.0)
    coeff = (-hot / group + 1.0 / (group * group) + GAMMA * cen / (scale_sq * root)) / (chips * 2)
    weighted = coeff * k_own
    z_own = zbuf[at, :]
    w_top = weighted.astype(BF16)
    w_low = (weighted - w_top.astype(F32)).astype(BF16)
    moved = dot(w_top, parts[:, 0:emb_w]) + dot(w_top, parts[:, emb_w:])
    moved = moved + dot(w_low, parts[:, 0:emb_w])
    grad = -(2.0 / spread) * (
        jnp.sum(weighted, axis=1, keepdims=True) * z_own
        - moved
    )
    ge = grad.astype(BF16)
    geT = jnp.transpose(ge.astype(F32)).astype(BF16)

    def backward(n, kk):
        gp = (dot(ge, PW[kk], ((1,), (1,))) / POS).astype(BF16)
        rows = dot(spread_mat, gp)
        gh = jnp.where(hid[kk].astype(F32) > 0.0, rows, 0.0).astype(BF16)
        conv_t = dot(featT[...], gh).astype(BF16)
        proj_t = dot(geT, pooled[kk]).astype(BF16)
        for half in range(2):
            cols = slice(half * 128, half * 128 + 128)
            term[n, half, 0:width] = conv_t[:, cols]
            term[n, half, width:] = proj_t[:, cols]

    order = [o for o in offsets if far(o)]
    order += [o for o in offsets[1:] if o[0] == 0 and o[1] in (1, X - 1)]
    order += [o for o in offsets[1:] if o not in order and o[1] == 0]
    order += [o for o in offsets[1:] if o not in order] + [offsets[0]]
    core_copies = {}
    relayed = {o: [] for o in offsets}
    group_copies = []

    def pair(n):
        o = order[n]
        core_copies[n].wait_recv()
        total = term[n, pl.ds(c, 1)][0].astype(F32) + core_in[n].astype(F32)
        for m, copy in relayed[o]:
            copy.wait_recv()
            total = total + group_in[m].astype(F32)
        pair_sum[n] = total.astype(BF16)
        if far(o):
            copy = send(pair_sum.at[n], group_in.at[n], dev_chip(to_chip(second_hop(o)), c))
            relayed[first_hop(o)].append((n, copy))
        elif n < len(order) - 1:
            copy = send(pair_sum.at[n], group_in.at[n], dev_chip(to_chip(o), c))
            group_copies.append((n, copy))

    for n, o in enumerate(order):
        backward(n, to_chip(o))
        core_copies[n] = send(term.at[n, 1 - c], core_in.at[n], other)
        if n:
            pair(n - 1)
    last = len(order) - 1
    pair(last)
    total = pair_sum[last].astype(F32)
    for n, copy in group_copies:
        copy.wait_recv()
        total = total + group_in[n].astype(F32)
    total = total.astype(BF16)
    span = 3 if reach else 1
    mid = span // 2
    piece = red0.shape[1]
    for p in range(Z + span - 1):
        q = (reach * p) % Z if reach else p
        red0[p] = total[q * piece : (q + 1) * piece]

    def position(j):
        return lax.rem(inverse * zmod(j) + Z - mid, Z)

    copies = []
    older = len(pending)
    for i, j in enumerate(close):
        copies.append(send(red0.at[pl.ds(position(j), span)], close_in.at[i], dev_z(j)))
    if reach:
        opposite = send(red0.at[lax.rem(inverse * zmod(8), Z)], opp_in, dev_z(8))
    sent(older)
    arrive(copies)
    total = red0[pl.ds(position(0), span)].astype(F32)
    for i in range(len(close)):
        total = total + close_in[i].astype(F32)
    if reach:
        red1[...] = total.astype(BF16)
        copies = [
            send(red1.at[0], reach_in.at[0], dev_z(-reach)),
            send(red1.at[2], reach_in.at[1], dev_z(reach)),
        ]
        opposite.wait_recv()
        total = total[mid] + opp_in[...].astype(F32)
        arrive(copies)
        total = total + reach_in[0].astype(F32) + reach_in[1].astype(F32)
    else:
        total = total[mid]
    red2[yh] = total.astype(BF16)
    copies = []
    older = len(pending)
    for j in range(1, YH):
        q = lax.rem(yh + j, YH)
        copies.append(send(red2.at[yh], red2.at[yh], dev_dp(q, zh, zl)))
    sent(older)
    arrive(copies)
    total = red2[0].astype(F32)
    for j in range(1, YH):
        total = total + red2[j].astype(F32)
    done[mid] = total.astype(BF16)
    if reach:
        copies = [
            send(done.at[1], done.at[0], dev_z(reach)),
            send(done.at[1], done.at[2], dev_z(-reach)),
        ]
        opposite = send(done.at[1], opp_done, dev_z(8))
    close_copies = []

    def pass_on(k):
        for i, j in enumerate(close):
            copy = send(done.at[k], close_done.at[i, k], dev_z(j))
            close_copies.append((i, j, k, copy))
        fin[zmod(reach * (k - mid))] = done[k]

    pass_on(mid)
    if reach:
        for k, copy in zip((0, 2), copies):
            copy.wait_recv()
            pass_on(k)
    if reach:
        opposite.wait_recv()
        fin[zmod(8)] = opp_done[...]
    for i, j, k, copy in close_copies:
        copy.wait_recv()
        fin[zmod(reach * (k - mid) - j)] = close_done[i, k]

    result = fin[...].astype(F32).reshape(width + emb_w, 128)
    oconv[...] = jnp.transpose(result[0:width])
    oproj[...] = jnp.transpose(result[width:])

    for copy in pending:
        copy.wait_send()


def local(features, shortcut, conv_weight, proj_weight, partner):
    rows, width = features.shape
    emb_w = proj_weight.shape[1]
    chips = YL * X
    dp = YH * ZH * ZL
    group = dp * 8
    both = width + emb_w
    Z = ZL * ZH
    piece = both // Z
    close, reach, _ = z_plan(Z)
    span = 3 if reach else 1
    sends = 120
    hbm = pl.BlockSpec(memory_space=pltpu.HBM)
    args = (features, shortcut, conv_weight, proj_weight, partner)
    args = [pltpu.with_memory_space_constraint(arg, pltpu.HBM) for arg in args]
    vmem = pl.BlockSpec(memory_space=pltpu.VMEM)
    grad_conv, grad_proj, loss = pl.pallas_call(
        kernel,
        out_shape=(
            jax.ShapeDtypeStruct((128, width), F32),
            jax.ShapeDtypeStruct((128, emb_w), F32),
            jax.ShapeDtypeStruct((1, 128), F32),
        ),
        in_specs=[hbm] * 5,
        out_specs=(vmem, vmem, vmem),
        scratch_shapes=[
            pltpu.VMEM((rows, width), BF16),
            pltpu.VMEM((rows, chips * 256), BF16),
            pltpu.VMEM((width, rows), BF16),
            pltpu.VMEM((chips, 256, width), BF16),
            pltpu.VMEM((chips, 256, emb_w), BF16),
            pltpu.VMEM((chips, rows, 256), BF16),
            pltpu.VMEM((chips, 8, 256), BF16),
            pltpu.VMEM((dp, 8, 128), F32),
            pltpu.VMEM((dp, 8, emb_w), F32),
            pltpu.VMEM((group, emb_w), F32),
            pltpu.VMEM((group, 2 * emb_w), BF16),
            pltpu.VMEM((group, 128), F32),
            pltpu.VMEM((group, group), F32),
            pltpu.VMEM((group, 128), F32),
            pltpu.VMEM((chips, 2, both, 128), BF16),
            pltpu.VMEM((chips, both, 128), BF16),
            pltpu.VMEM((chips, both, 128), BF16),
            pltpu.VMEM((chips, both, 128), BF16),
            pltpu.VMEM((Z + span - 1, piece, 128), BF16),
            pltpu.VMEM((len(close) or 1, span, piece, 128), BF16),
            pltpu.VMEM((span, piece, 128), BF16),
            pltpu.VMEM((2, piece, 128), BF16),
            pltpu.VMEM((piece, 128), BF16),
            pltpu.VMEM((YH, piece, 128), BF16),
            pltpu.VMEM((span, piece, 128), BF16),
            pltpu.VMEM((len(close) or 1, span, piece, 128), BF16),
            pltpu.VMEM((piece, 128), BF16),
            pltpu.VMEM((Z, piece, 128), BF16),
            pltpu.SMEM((8,), jnp.int32),
            pltpu.SemaphoreType.DMA((5,)),
            pltpu.SemaphoreType.DMA((sends,)),
            pltpu.SemaphoreType.DMA((sends,)),
        ],
        compiler_params=pltpu.CompilerParams(
            collective_id=0, has_side_effects=True, vmem_limit_bytes=48 << 20
        ),
    )(*args)
    return grad_conv, grad_proj, loss[0, 0:1]


def solution(mesh):
    return jax.shard_map(
        local,
        mesh=mesh,
        in_specs=(
            P(("dp", "fsdp"), None),
            P(("dp", "fsdp"), None),
            P("fsdp", None),
            P("fsdp", None),
            P(("dp", "fsdp")),
        ),
        out_specs=(P("fsdp", None), P("fsdp", None), P("fsdp")),
        check_vma=False,
    )
```

```python
import jax
import jax.numpy as jnp
from jax import lax
from jax.experimental import pallas as pl
from jax.experimental.pallas import tpu as pltpu
from jax.sharding import PartitionSpec as P

MESH = pl.DeviceIdType.MESH
BF16 = jnp.bfloat16
F32 = jnp.float32

POS = 49
GAMMA = 3.0
EPSILON = 1e-06

YH, ZH, ZL = 4, 4, 4
YL, X = 2, 4


def far(o):
    return o[0] > 0 and o[1] > 0


def first_hop(o):
    return (o[0], 0) if o[1] in (1, X - 1) else (0, o[1])


def second_hop(o):
    return (0, o[1]) if o[1] in (1, X - 1) else (o[0], 0)


def z_plan(n):
    if n == 16:
        return [1, -1, 2, -2], 5, 13
    return near(n), 0, 1


def near(n):
    return [j if j <= n // 2 else j - n for j in sorted(range(1, n), key=lambda j: min(j, n - j))]


def dot(a, b, dims=((1,), (0,)), precision=None):
    return lax.dot_general(
        a, b, (dims, ((), ())), precision=precision, preferred_element_type=F32
    )


def kernel(
    feat_h, short_h, conv_h, proj_h, partner_h,
    oconv, oproj, oloss,
    feat, short, featT, W, PW, hid, pooled, part, emb, zbuf, parts, sqs, kmat, rcol,
    term, core_in, pair_sum, group_in,
    red0, close_in, red1, reach_in, opp_in, red2, done, close_done, opp_done, fin,
    partner_s, lsem, ssem, rsem,
):
    chips = YL * X
    dp = YH * ZH * ZL
    images = 8
    width = feat.shape[1]
    emb_w = emb.shape[2]
    group = dp * images

    d = lax.axis_index("dp")
    f = lax.axis_index("fsdp")
    yh = lax.div(d, ZH * ZL)
    zh = lax.rem(lax.div(d, ZL), ZH)
    zl = lax.rem(d, ZL)
    chip = lax.div(f, 2)
    yl = lax.div(chip, X)
    x = lax.rem(chip, X)
    c = lax.rem(f, 2)

    def dev_chip(ch, core):
        return (d, ch * 2 + core)

    def dev_dp(a, b, e):
        return ((a * ZH + b) * ZL + e, f)

    used = [0]
    pending = []

    def send(src, dst, dev):
        i = used[0]
        used[0] += 1
        copy = pltpu.make_async_remote_copy(
            src_ref=src, dst_ref=dst, send_sem=ssem.at[i], recv_sem=rsem.at[i],
            device_id=dev, device_id_type=MESH,
        )
        copy.start()
        pending.append(copy)
        return copy

    def sent(n):
        for copy in pending[:n]:
            copy.wait_send()
        del pending[:n]

    offsets = [(dy, dx) for dy in range(YL) for dx in range(X)]
    offsets.sort(key=lambda o: (far(o), o[0] + min(o[1], X - o[1]), -o[0]))

    def to_chip(o):
        return lax.rem(yl + o[0], YL) * X + lax.rem(x + o[1], X)

    def from_chip(o):
        return lax.rem(yl + YL - o[0], YL) * X + lax.rem(x + X - o[1], X)

    peers = [dev_chip(chip, 1 - c)]
    peers += [dev_chip(to_chip(o), c) for o in offsets[1:] if not far(o)]
    peers += [dev_dp(lax.rem(yh + j, YH), zh, zl) for j in range(1, YH)]
    Z = ZH * ZL
    z = zh * ZL + zl

    def zmod(j):
        return lax.rem(z + j + Z, Z)

    def dev_z(j):
        return (yh * Z + zmod(j), f)

    near_z = near(ZL)
    close, reach, inverse = z_plan(Z)
    steps = near_z + close + [j * ZL for j in range(1, ZH)] + ([reach, 8] if reach else [])
    steps = {j % Z for j in steps} | {-j % Z for j in steps}
    peers += [dev_z(j) for j in sorted(steps, key=lambda j: min(j, Z - j))]
    barrier = pltpu.get_barrier_semaphore()
    for peer in reversed(peers):
        pl.semaphore_signal(barrier, inc=1, device_id=peer, device_id_type=MESH)

    mine = pl.ds(pl.multiple_of(c * 128, 128), 128)
    local = [
        pltpu.make_async_copy(conv_h, W.at[chip, mine], lsem.at[0]),
        pltpu.make_async_copy(feat_h, feat, lsem.at[1]),
        pltpu.make_async_copy(short_h, short, lsem.at[2]),
        pltpu.make_async_copy(proj_h, PW.at[chip, mine], lsem.at[3]),
        pltpu.make_async_copy(partner_h, partner_s, lsem.at[4]),
    ]
    for copy in local:
        copy.start()

    slot = (zl * YH + yh) * ZH + zh
    row8 = lax.broadcasted_iota(jnp.int32, (images, 128), 0)
    local[4].wait()
    column = jnp.zeros((images, 128), jnp.int32)
    for i in range(images):
        column = jnp.where(row8 == i, partner_s[i], column)
    part[pl.ds(slot, 1)] = column.astype(F32)[None]

    pl.semaphore_wait(barrier, len(peers))

    other = dev_chip(chip, 1 - c)

    def block(ref, ch):
        return ref.at[ch, mine]

    def start_gather(source, ref):
        direct = {}
        for o in offsets[1:]:
            if not far(o):
                direct[o] = send(source, block(ref, chip), dev_chip(to_chip(o), c))
        return direct, {offsets[0]: send(source, block(ref, chip), other)}

    def landed(ref, o, direct, paired):
        direct[o].wait_recv()
        view = block(ref, from_chip(o))
        for p in offsets:
            if far(p) and first_hop(p) == o:
                direct[p] = send(view, view, dev_chip(to_chip(second_hop(p)), c))
        paired[o] = send(view, view, other)

    conv_direct, conv_pair = start_gather(conv_h, W)

    def arrive(copies):
        for copy in copies:
            copy.wait_recv()

    def far_stage(buf):
        view = buf.at[pl.ds(slot, 1)]
        return [send(view, view, dev_dp(yh, lax.rem(zh + j, ZH), zl)) for j in range(1, ZH)]

    def row(buf, y):
        return buf.at[pl.ds((zl * YH + y) * ZH, ZH)]

    def y_stage(buf):
        view = row(buf, yh)
        return {
            j: send(view, view, dev_dp(lax.rem(yh + j + YH, YH), zh, zl)) for j in near(YH)
        }

    def near_stage(view):
        return [send(view, view, dev_z(j)) for j in near_z]

    part_copies = far_stage(part)

    ri = lax.broadcasted_iota(jnp.int32, (images, images * POS), 1)
    ii = lax.broadcasted_iota(jnp.int32, (images, images * POS), 0)
    pool_mat = jnp.where((ri >= ii * POS) & (ri < ii * POS + POS), 1.0, 0.0).astype(BF16)
    ri = lax.broadcasted_iota(jnp.int32, (images * POS, images), 0)
    ii = lax.broadcasted_iota(jnp.int32, (images * POS, images), 1)
    spread_mat = jnp.where((ri >= ii * POS) & (ri < ii * POS + POS), 1.0, 0.0).astype(BF16)

    def lanes(kk):
        return pl.ds(pl.multiple_of(kk * 256, 256), 256)

    def forward(kk):
        pre = dot(feat[...], W[kk], ((1,), (1,))) + short[:, lanes(kk)].astype(F32)
        h = jnp.maximum(pre, 0.0)
        hi = h.astype(BF16)
        low = (h - hi.astype(F32)).astype(BF16)
        hid[kk] = hi
        total = dot(pool_mat, hi) + dot(pool_mat, low)
        pooled[kk] = (total / POS).astype(BF16)

    for copy in local[:3]:
        copy.wait()
    proj_direct = proj_pair = None
    for n, o in enumerate(offsets):
        if n:
            landed(W, o, conv_direct, conv_pair)
            if n == 1:
                proj_direct, proj_pair = start_gather(proj_h, PW)
            last = offsets[n - 1]
            conv_pair[last].wait_recv()
            forward(from_chip(last))
        if n == min(1, chips - 1):
            featT[...] = jnp.transpose(feat[...].astype(F32)).astype(BF16)
    if chips == 1:
        proj_direct, proj_pair = start_gather(proj_h, PW)
    arrive(part_copies)
    part_copies = y_stage(part)
    for o in offsets[1:]:
        landed(PW, o, proj_direct, proj_pair)
    conv_pair[offsets[-1]].wait_recv()
    forward(from_chip(offsets[-1]))
    local[3].wait()
    arrive(part_copies.values())
    part_copies = near_stage(part.at[pl.ds(zl * YH * ZH, YH * ZH)])

    own = jnp.zeros((images, emb_w), F32)
    for o in offsets:
        proj_pair[o].wait_recv()
        kk = from_chip(o)
        own = own + dot(pooled[kk], PW[kk])

    emb[pl.ds(slot, 1)] = own[None]
    def to_y(zq):
        view = emb.at[pl.ds((zl * YH + yh) * ZH + zq, 1)]
        for j in near(YH):
            y_copies[j].append(send(view, view, dev_dp(lax.rem(yh + j + YH, YH), zh, zl)))

    y_copies = {j: [] for j in near(YH)}
    older = len(pending)
    far_copies = dict(zip(range(1, ZH), far_stage(emb)))
    to_y(zh)
    sent(older)
    for j in near(ZH):
        far_copies[j % ZH].wait_recv()
        to_y(lax.rem(zh - j + ZH, ZH))
    copies = near_stage(row(emb, yh))
    for j, landed_y in y_copies.items():
        arrive(landed_y)
        copies += near_stage(row(emb, lax.rem(yh - j + YH, YH)))
    arrive(copies)
    arrive(part_copies)

    zall = emb[...].reshape(group, emb_w)
    center = jnp.mean(zall, axis=0, keepdims=True)
    zc = zall - center
    zbuf[...] = zc
    top = zc.astype(BF16)
    parts[:, 0:emb_w] = top
    parts[:, emb_w:] = (zc - top.astype(F32)).astype(BF16)
    sq_col = jnp.sum(zc * zc, axis=1, keepdims=True)
    spread = 2.0 * jnp.sum(sq_col) / group
    sq_wide = jnp.broadcast_to(sq_col, (group, 128))
    sqs[...] = sq_wide
    sq_row = jnp.transpose(sq_wide)[0:1]
    lane = lax.broadcasted_iota(jnp.int32, (1, group), 1)
    ls = lane // images
    lzl = ls // (YH * ZH)
    lyh = (ls // ZH) % YH
    lzh = ls % ZH
    member = (((lyh * ZH + lzh) * ZL + lzl) * images + lane % images).astype(F32)

    step = 256 if group % 256 == 0 else group
    scale = 1.0 / (2.0 * spread)

    def kernel_rows(i, carry):
        col_sum, positive = carry
        rows = pl.ds(pl.multiple_of(i * (step // images), step // images), step // images)
        at = pl.ds(pl.multiple_of(i * step, step), step)
        zt, zm = parts[at, 0:emb_w], parts[at, emb_w:]
        inner = dot(jnp.concatenate([zt, zt], axis=1), parts[...], ((1,), (1,)))
        inner = inner + dot(zm, parts[:, 0:emb_w], ((1,), (1,)))
        kk = jnp.exp(-(sqs[at, 0:1] + sq_row - 2.0 * inner) * scale)
        kmat[at, :] = kk
        rcol[at, :] = jnp.broadcast_to(jnp.mean(kk, axis=1, keepdims=True), (step, 128))
        who = part[rows].reshape(step, 128)[:, 0:1]
        positive = positive + jnp.sum(jnp.where(who == member, kk, 0.0), axis=0, keepdims=True)
        return col_sum + jnp.sum(kk, axis=0, keepdims=True), positive

    zero = jnp.zeros((1, group), F32)
    col_sum, positive = lax.fori_loop(0, group // step, kernel_rows, (zero, zero))
    row_mean = col_sum / group
    t = jnp.sum(row_mean) / group

    def square_rows(i, carry):
        at = pl.ds(pl.multiple_of(i * step, step), step)
        cen = kmat[at, :] - rcol[at, 0:1] - row_mean + t
        return carry + jnp.sum(cen * cen, axis=0, keepdims=True)

    sums = lax.fori_loop(0, group // step, square_rows, zero)
    scale_sq = float(group - 1) ** 2
    root_v = jnp.sqrt(jnp.broadcast_to(jnp.sum(sums) / scale_sq + EPSILON, (1, 128)))
    loss = -(jnp.sum(positive) / group - t) + GAMMA * root_v
    oloss[...] = loss
    root = root_v[0:1, 0:1]

    at = pl.ds(pl.multiple_of(slot * images, images), images)
    k_own = kmat[at, :]
    cen = k_own - rcol[at, 0:1] - row_mean + t
    who = part[pl.ds(slot, 1)].reshape(images, 128)[:, 0:1]
    hot = jnp.where(who == member, 1.0, 0.0)
    coeff = (-hot / group + 1.0 / (group * group) + GAMMA * cen / (scale_sq * root)) / (chips * 2)
    weighted = coeff * k_own
    z_own = zbuf[at, :]
    w_top = weighted.astype(BF16)
    w_low = (weighted - w_top.astype(F32)).astype(BF16)
    moved = dot(w_top, parts[:, 0:emb_w]) + dot(w_top, parts[:, emb_w:])
    moved = moved + dot(w_low, parts[:, 0:emb_w])
    grad = -(2.0 / spread) * (
        jnp.sum(weighted, axis=1, keepdims=True) * z_own
        - moved
    )
    ge = grad.astype(BF16)
    geT = jnp.transpose(ge.astype(F32)).astype(BF16)

    def backward(n, kk):
        gp = (dot(ge, PW[kk], ((1,), (1,))) / POS).astype(BF16)
        rows = dot(spread_mat, gp)
        gh = jnp.where(hid[kk].astype(F32) > 0.0, rows, 0.0).astype(BF16)
        conv_t = dot(featT[...], gh).astype(BF16)
        proj_t = dot(geT, pooled[kk]).astype(BF16)
        for half in range(2):
            cols = slice(half * 128, half * 128 + 128)
            term[n, half, 0:width] = conv_t[:, cols]
            term[n, half, width:] = proj_t[:, cols]

    order = [o for o in offsets if far(o)]
    order += [o for o in offsets[1:] if o[0] == 0 and o[1] in (1, X - 1)]
    order += [o for o in offsets[1:] if o not in order and o[1] == 0]
    order += [o for o in offsets[1:] if o not in order] + [offsets[0]]
    core_copies = {}
    relayed = {o: [] for o in offsets}
    group_copies = []

    def pair(n):
        o = order[n]
        core_copies[n].wait_recv()
        total = term[n, pl.ds(c, 1)][0].astype(F32) + core_in[n].astype(F32)
        for m, copy in relayed[o]:
            copy.wait_recv()
            total = total + group_in[m].astype(F32)
        pair_sum[n] = total.astype(BF16)
        if far(o):
            copy = send(pair_sum.at[n], group_in.at[n], dev_chip(to_chip(second_hop(o)), c))
            relayed[first_hop(o)].append((n, copy))
        elif n < len(order) - 1:
            copy = send(pair_sum.at[n], group_in.at[n], dev_chip(to_chip(o), c))
            group_copies.append((n, copy))

    for n, o in enumerate(order):
        backward(n, to_chip(o))
        core_copies[n] = send(term.at[n, 1 - c], core_in.at[n], other)
        if n:
            pair(n - 1)
    last = len(order) - 1
    pair(last)
    total = pair_sum[last].astype(F32)
    for n, copy in group_copies:
        copy.wait_recv()
        total = total + group_in[n].astype(F32)
    total = total.astype(BF16)
    span = 3 if reach else 1
    mid = span // 2
    piece = red0.shape[1]
    for p in range(Z + span - 1):
        q = (reach * p) % Z if reach else p
        red0[p] = total[q * piece : (q + 1) * piece]

    def position(j):
        return lax.rem(inverse * zmod(j) + Z - mid, Z)

    copies = []
    older = len(pending)
    for i, j in enumerate(close):
        copies.append(send(red0.at[pl.ds(position(j), span)], close_in.at[i], dev_z(j)))
    if reach:
        opposite = send(red0.at[lax.rem(inverse * zmod(8), Z)], opp_in, dev_z(8))
    sent(older)
    arrive(copies)
    total = red0[pl.ds(position(0), span)].astype(F32)
    for i in range(len(close)):
        total = total + close_in[i].astype(F32)
    if reach:
        red1[...] = total.astype(BF16)
        copies = [
            send(red1.at[0], reach_in.at[0], dev_z(-reach)),
            send(red1.at[2], reach_in.at[1], dev_z(reach)),
        ]
        opposite.wait_recv()
        total = total[mid] + opp_in[...].astype(F32)
        arrive(copies)
        total = total + reach_in[0].astype(F32) + reach_in[1].astype(F32)
    else:
        total = total[mid]
    red2[yh] = total.astype(BF16)
    copies = []
    older = len(pending)
    for j in range(1, YH):
        q = lax.rem(yh + j, YH)
        copies.append(send(red2.at[yh], red2.at[yh], dev_dp(q, zh, zl)))
    sent(older)
    arrive(copies)
    total = red2[0].astype(F32)
    for j in range(1, YH):
        total = total + red2[j].astype(F32)
    done[mid] = total.astype(BF16)
    if reach:
        copies = [
            send(done.at[1], done.at[0], dev_z(reach)),
            send(done.at[1], done.at[2], dev_z(-reach)),
        ]
        opposite = send(done.at[1], opp_done, dev_z(8))
    close_copies = []

    def pass_on(k):
        for i, j in enumerate(close):
            copy = send(done.at[k], close_done.at[i, k], dev_z(j))
            close_copies.append((i, j, k, copy))
        fin[zmod(reach * (k - mid))] = done[k]

    pass_on(mid)
    if reach:
        for k, copy in zip((0, 2), copies):
            copy.wait_recv()
            pass_on(k)
    if reach:
        opposite.wait_recv()
        fin[zmod(8)] = opp_done[...]
    for i, j, k, copy in close_copies:
        copy.wait_recv()
        fin[zmod(reach * (k - mid) - j)] = close_done[i, k]

    result = fin[...].astype(F32).reshape(width + emb_w, 128)
    oconv[...] = jnp.transpose(result[0:width])
    oproj[...] = jnp.transpose(result[width:])

    for copy in pending:
        copy.wait_send()


def local(features, shortcut, conv_weight, proj_weight, partner):
    rows, width = features.shape
    emb_w = proj_weight.shape[1]
    chips = YL * X
    dp = YH * ZH * ZL
    group = dp * 8
    both = width + emb_w
    Z = ZL * ZH
    piece = both // Z
    close, reach, _ = z_plan(Z)
    span = 3 if reach else 1
    sends = 120
    hbm = pl.BlockSpec(memory_space=pltpu.HBM)
    args = (features, shortcut, conv_weight, proj_weight, partner)
    args = [pltpu.with_memory_space_constraint(arg, pltpu.HBM) for arg in args]
    vmem = pl.BlockSpec(memory_space=pltpu.VMEM)
    grad_conv, grad_proj, loss = pl.pallas_call(
        kernel,
        out_shape=(
            jax.ShapeDtypeStruct((128, width), F32),
            jax.ShapeDtypeStruct((128, emb_w), F32),
            jax.ShapeDtypeStruct((1, 128), F32),
        ),
        in_specs=[hbm] * 5,
        out_specs=(vmem, vmem, vmem),
        scratch_shapes=[
            pltpu.VMEM((rows, width), BF16),
            pltpu.VMEM((rows, chips * 256), BF16),
            pltpu.VMEM((width, rows), BF16),
            pltpu.VMEM((chips, 256, width), BF16),
            pltpu.VMEM((chips, 256, emb_w), BF16),
            pltpu.VMEM((chips, rows, 256), BF16),
            pltpu.VMEM((chips, 8, 256), BF16),
            pltpu.VMEM((dp, 8, 128), F32),
            pltpu.VMEM((dp, 8, emb_w), F32),
            pltpu.VMEM((group, emb_w), F32),
            pltpu.VMEM((group, 2 * emb_w), BF16),
            pltpu.VMEM((group, 128), F32),
            pltpu.VMEM((group, group), F32),
            pltpu.VMEM((group, 128), F32),
            pltpu.VMEM((chips, 2, both, 128), BF16),
            pltpu.VMEM((chips, both, 128), BF16),
            pltpu.VMEM((chips, both, 128), BF16),
            pltpu.VMEM((chips, both, 128), BF16),
            pltpu.VMEM((Z + span - 1, piece, 128), BF16),
            pltpu.VMEM((len(close) or 1, span, piece, 128), BF16),
            pltpu.VMEM((span, piece, 128), BF16),
            pltpu.VMEM((2, piece, 128), BF16),
            pltpu.VMEM((piece, 128), BF16),
            pltpu.VMEM((YH, piece, 128), BF16),
            pltpu.VMEM((span, piece, 128), BF16),
            pltpu.VMEM((len(close) or 1, span, piece, 128), BF16),
            pltpu.VMEM((piece, 128), BF16),
            pltpu.VMEM((Z, piece, 128), BF16),
            pltpu.SMEM((8,), jnp.int32),
            pltpu.SemaphoreType.DMA((5,)),
            pltpu.SemaphoreType.DMA((sends,)),
            pltpu.SemaphoreType.DMA((sends,)),
        ],
        compiler_params=pltpu.CompilerParams(
            collective_id=0, has_side_effects=True, vmem_limit_bytes=48 << 20
        ),
    )(*args)
    return grad_conv, grad_proj, loss[0, 0:1]


def solution(mesh):
    return jax.shard_map(
        local,
        mesh=mesh,
        in_specs=(
            P(("dp", "fsdp"), None),
            P(("dp", "fsdp"), None),
            P("fsdp", None),
            P("fsdp", None),
            P(("dp", "fsdp")),
        ),
        out_specs=(P("fsdp", None), P("fsdp", None), P("fsdp")),
        check_vma=False,
    )
```
